256 devices in a mesh: seq: 64 (over z, x, core), head: 4 (over y).
Axes of the slice: x: 4, y: 4, z: 8, core: 2. Of those that a mesh axis runs over, the one named last changes fastest.
Arguments:
- queries: bfloat16 [16384, 4096], P('seq', 'head'), may hold values from -6 to 6
- key_rows: bfloat16 [16384, 4096], P('seq', 'head'), may hold values from -18 to 18
- values: bfloat16 [16384, 4096], P('seq', 'head'), may hold values from -6 to 6
- write_gate: float32 [16384, 32], P('seq', 'head'), may hold values from 0.05 to 1
- ridge_diag: float32 [32, 128], P('head'), may hold values from 0.1 to 4
- norm_gain: float32 [4096], replicated, may hold values from 0.5 to 1.5
- gate_logits: bfloat16 [16384, 4096], P(('seq', 'head')), may hold values from -8 to 8
Outputs:
- layer_out: bfloat16 [16384, 4096], P(('seq', 'head'))
The draws below stay inside these ranges and needn't reach their ends.
All inputs are finite; a program needn't handle non-finite values.
Results may differ from the reference program's by a relative error of at most 0.018.
Values may be sent and summed in bfloat16 or wider, within the bound.
A program may use at most 128 MiB of HBM per device.

```python
import math
import jax
import jax.numpy as jnp
from jax import lax

HEADS = 32
DH = 128
D = 4096
TOK_DEV = 256
ITERS = 8
TOKENS = 16384


def draw_key_rows(key, part):
    key_scale = jax.random.fold_in(key, 11)
    key_base = jax.random.fold_in(key, 12)
    scales = jnp.exp(jax.random.uniform(key_scale, (HEADS * DH,), jnp.float32, math.log(0.1), math.log(3.0)))
    base = jax.random.truncated_normal(key_base, -6.0, 6.0, (TOKENS, HEADS * DH), jnp.float32)
    return (base * scales[None, :]).astype(jnp.bfloat16)


def steps_of(own_key, dims, pieces, smallest, high):
    loudness = 1.0
    for axis_at, shards_of in pieces:
        draws = jax.random.uniform(jax.random.fold_in(jax.random.fold_in(own_key, 6), axis_at), (shards_of,), jnp.float32, smallest / len(pieces), high / len(pieces))
        loudness = loudness * jnp.repeat(jnp.exp(draws), dims[axis_at] // shards_of).reshape((-1,) + (1,) * (len(dims) - 1 - axis_at))
    return loudness


def centred(key, extent, spread, most, cuts=(), dtype=jnp.bfloat16):
    values = spread * jax.random.normal(key, extent, jnp.float32)
    if cuts:
        values = values * steps_of(key, extent, cuts, -0.22, 0.18)
    return jnp.clip(values, -most, most).astype(dtype)


def setup_inputs(seed: int = 0) -> dict:
    arg_keys = jax.random.split(jax.random.key(seed), 8)
    queries = centred(arg_keys[0], (TOKENS, D), 1.0, 6.0, ((0, 64), (1, 4)))
    key_rows = draw_key_rows(jax.random.fold_in(arg_keys[7], 71), 0)
    values = centred(arg_keys[2], (TOKENS, D), 1.0, 6.0, ((0, 64), (1, 4)))
    write_gate = jnp.clip(0.05 + 0.95 * jax.random.uniform(arg_keys[3], (TOKENS, HEADS), jnp.float32) ** steps_of(arg_keys[3], (TOKENS, HEADS), ((0, 64), (1, 4)), -0.2, 0.2), 0.05, 1.0)
    ridge_diag = jnp.clip(jnp.exp(math.log(4.0) - 3.6888794 * jax.random.uniform(arg_keys[4], (HEADS, DH), jnp.float32) ** steps_of(arg_keys[4], (HEADS, DH), ((0, 4),), -0.2, 0.2)), 0.1, 4.0)
    norm_gain = jnp.clip(1.0 + 0.1 * jax.random.normal(arg_keys[5], (D,), jnp.float32), 0.5, 1.5)
    gate_logits = centred(arg_keys[6], (TOKENS, D), 2.0, 8.0, ((0, 256),))
    return {"queries": queries, "key_rows": key_rows, "values": values, "write_gate": write_gate, "ridge_diag": ridge_diag, "norm_gain": norm_gain, "gate_logits": gate_logits}


precise = lax.Precision.HIGHEST

def normalize(block):
    return block * lax.rsqrt(lax.optimization_barrier(jnp.sum(block * block, axis=-1, keepdims=True)) + 1e-06)

def one_head(inputs):
    query_n, key_n, value_f, gate_h, ridge_h = inputs
    count = TOKENS // TOK_DEV
    query_b = query_n.reshape(count, TOK_DEV, DH)
    key_b = key_n.reshape(count, TOK_DEV, DH)
    value_b = value_f.reshape(count, TOK_DEV, DH)
    gate_b = gate_h.reshape(count, TOK_DEV)
    causal = jnp.arange(TOK_DEV)[:, None] >= jnp.arange(TOK_DEV)[None, :]

    def step(carry, block):
        state_kk, state_vk = carry
        q_blk, k_blk, v_blk, g_blk = block
        weights = jnp.where(causal, g_blk[None, :], jnp.float32(0.0))

        def apply(direction):
            scores = jnp.dot(direction, k_blk.T, precision=precise)
            inner = jnp.dot(weights * scores, k_blk, precision=precise)
            return jnp.dot(direction, state_kk, precision=precise) + inner + ridge_h[None, :] * direction
        iterate = jnp.zeros_like(q_blk)
        residual = q_blk
        direction = q_blk
        norm_now = lax.optimization_barrier(jnp.sum(residual * residual, axis=-1, keepdims=True))
        for sweep in range(ITERS):
            image = apply(direction)
            alpha = norm_now / lax.optimization_barrier(jnp.sum(direction * image, axis=-1, keepdims=True))
            iterate = iterate + alpha * direction
            residual = residual - alpha * image
            norm_next = lax.optimization_barrier(jnp.sum(residual * residual, axis=-1, keepdims=True))
            direction = residual + norm_next / norm_now * direction
            norm_now = norm_next
        scores = jnp.dot(iterate, k_blk.T, precision=precise)
        result = jnp.dot(iterate, state_vk.T, precision=precise) + jnp.dot(weights * scores, v_blk, precision=precise)
        state_kk = state_kk + jnp.dot((k_blk * g_blk[:, None]).T, k_blk, precision=precise)
        state_vk = state_vk + jnp.dot((v_blk * g_blk[:, None]).T, k_blk, precision=precise)
        return ((state_kk, state_vk), result)
    empty_state = jnp.zeros((DH, DH), jnp.float32)
    unused, results = lax.scan(step, (empty_state, empty_state), (query_b, key_b, value_b, gate_b))
    return results.reshape(TOKENS, DH)

def reference(queries, key_rows, values, write_gate, ridge_diag, norm_gain, gate_logits):

    def split_heads(block):
        return block.astype(jnp.float32).reshape(TOKENS, HEADS, DH).transpose(1, 0, 2)
    query_n = normalize(split_heads(queries))
    key_n = normalize(split_heads(key_rows))
    value_f = split_heads(values)
    results = lax.map(one_head, (query_n, key_n, value_f, write_gate.T, ridge_diag))
    mesa_out = results.transpose(1, 0, 2).reshape(TOKENS, HEADS * DH).astype(jnp.bfloat16)
    wide_rows = lax.optimization_barrier(mesa_out).astype(jnp.float32)
    factor = lax.rsqrt(lax.optimization_barrier(jnp.mean(wide_rows * wide_rows, axis=-1, keepdims=True)) + 1e-06)
    gated = wide_rows * factor * norm_gain[None, :] * jax.nn.sigmoid(gate_logits.astype(jnp.float32))
    return gated.astype(jnp.bfloat16)
```

```python
import functools

import jax
import jax.numpy as jnp
from jax import lax
from jax.experimental import pallas as pl
from jax.experimental.pallas import tpu as pltpu
from jax.sharding import PartitionSpec as P

MESH = pl.DeviceIdType.MESH
f32, bf16 = jnp.float32, jnp.bfloat16
ITERS = 8
HEADS = 8
DH = 128
TOK = 256
ROW = 8
COL = 8
Y = 4
ROWS_OUT = TOK // Y
EPS = 1e-6
GROUP = 4


def dot(a, b):
    return jnp.dot(a, b, preferred_element_type=f32)


def sums(x):
    return jnp.sum(x, axis=0, keepdims=True)


def split(x):
    hi = x.astype(bf16)
    return hi, (x - hi.astype(f32)).astype(bf16)


def stack(x):
    return jnp.concatenate(split(x), axis=0)


def iota(shape, axis):
    return lax.broadcasted_iota(jnp.int32, shape, axis)


def weigh(scores, top_left, top_right, bottom_right):
    top = jnp.concatenate([scores[0:128, 0:128] * top_left, scores[0:128, 128:256] * top_right], axis=1)
    bottom = jnp.concatenate([jnp.zeros((128, 128), f32), scores[128:256, 128:256] * bottom_right], axis=1)
    return jnp.concatenate([top, bottom], axis=0)


def diag_rows(d):
    hi = d.astype(bf16).astype(f32)
    row = iota((16, 128), 0)
    return jnp.where(row == 0, hi, jnp.where(row == 1, d - hi, 0.0)).astype(bf16)


def diag_of(rows):
    return rows[0:1] + rows[1:2]


def kernel(
    q, k, v, wg, ridge, gain, gate, out,
    keys2, mix, kt, vt, w, cvb, r, p, x, rr, dgb, sg, mesa, full,
    snd_k, row_k, ebuf_k, cs_k, cr_k, zs_k, zr_k, s4_k, all_k,
    snd_v, row_v, ebuf_v, cs_v, cr_v, zs_v, zr_v, s4_v, all_v,
    ssem, rsem, ysend, yrecv,
):
    seq, y = lax.axis_index("seq"), lax.axis_index("head")
    z, me = seq // ROW, seq % ROW

    def row_peer(i):
        return (me + i) % ROW

    def col_peer(i):
        return (z + i) % COL

    barrier = pltpu.get_barrier_semaphore()
    for i in range(1, ROW):
        pl.semaphore_signal(barrier, inc=1, device_id=(z * ROW + row_peer(i), y), device_id_type=MESH)
    for i in range(1, COL):
        pl.semaphore_signal(barrier, inc=1, device_id=(col_peer(i) * ROW + me, y), device_id_type=MESH)
    for i in range(1, Y):
        pl.semaphore_signal(barrier, inc=1, device_id=(seq, (y + i) % Y), device_id_type=MESH)

    started = []

    def send(stage, i, src, dst, in_row):
        to = z * ROW + row_peer(i) if in_row else col_peer(i) * ROW + me
        copy = pltpu.make_async_remote_copy(
            src_ref=src,
            dst_ref=dst,
            send_sem=ssem.at[stage, i - 1],
            recv_sem=rsem.at[stage, i - 1],
            device_id=(to, y),
            device_id_type=MESH,
        )
        copy.start()
        started.append(copy)
        return copy

    eye = iota((128, 128), 0) == iota((128, 128), 1)
    tri = iota((128, 128), 0) <= iota((128, 128), 1)
    lane8 = iota((TOK, HEADS), 1)

    wait_k1, wait_v1 = [], []
    for i in list(range(1, ROW)) + [0]:
        h = row_peer(i)
        cols = pl.ds(pl.multiple_of(h * DH, DH), DH)
        kb = k[:, cols]
        k32 = kb.astype(f32)
        inv = lax.rsqrt(jnp.sum(k32 * k32, axis=1, keepdims=True) + EPS)
        b = jnp.sum(jnp.where(lane8 == h, wg[...], 0.0), axis=1, keepdims=True)
        cv = b * inv
        c = cv * inv
        k_t = k32.T.astype(bf16)
        state = dot(k_t, (k32 * c).astype(bf16))
        snd_k[h, 0:128] = jnp.where(eye, 0.0, state).astype(bf16)
        snd_k[h, 128:144] = diag_rows(sums(jnp.where(eye, state, 0.0)))
        if i == 1:
            pl.semaphore_wait(barrier, ROW + COL + Y - 3)
        if i:
            wait_k1.append(send(0, i, snd_k.at[h], row_k.at[me], True))
        else:
            row_k[me] = snd_k[me]
        keys2[h, :, 0:128] = kb
        keys2[h, :, 128:256] = kb
        kt[h] = k_t
        w[h, 0] = jnp.where(tri, c[0:128], 0.0)
        w[h, 1] = jnp.broadcast_to(c[0:128], (128, 128))
        w[h, 2] = jnp.where(tri, c[128:256], 0.0)
        cvb[h] = jnp.broadcast_to(cv, (TOK, DH))
    for i in list(range(1, ROW)) + [0]:
        h = row_peer(i)
        cols = pl.ds(pl.multiple_of(h * DH, DH), DH)
        v_t = v[:, cols].astype(f32).T.astype(bf16)
        vt[h] = v_t
        snd_v[h] = dot(v_t, (k[:, cols].astype(f32) * cvb[h]).astype(bf16)).astype(bf16)
        if i:
            wait_v1.append(send(1, i, snd_v.at[h], row_v.at[me], True))
        else:
            row_v[me] = snd_v[me]

    def row_sums(waits, rows, ebuf, pieces, landed, stage, with_diag):
        for copy in waits:
            copy.wait_recv()
        total = jnp.zeros(ebuf.shape[1:], f32)
        for s in range(ROW):
            ebuf[s] = total
            total = total + rows[s].astype(f32)
        for j in range(COL):
            pieces[j, 0:16] = total[16 * j : 16 * j + 16].astype(bf16)
            if with_diag:
                pieces[j, 16:32] = diag_rows(diag_of(total[128:144]))
        landed[z] = pieces[z]
        return [send(stage, i, pieces.at[col_peer(i)], landed.at[z], False) for i in range(1, COL)]

    def col_sums(waits, landed, zs, zr, stage):
        for copy in waits:
            copy.wait_recv()
        total = jnp.zeros((16, 128), f32)
        for s in range(COL):
            zs[s] = total.astype(bf16)
            total = total + landed[s, 0:16].astype(f32)
        zr[z] = zs[z]
        return [send(stage, i, zs.at[col_peer(i)], zr.at[z], False) for i in range(1, COL)]

    def hand_out(waits, zr, ebuf, s4, everything, stage, diag):
        for copy in waits:
            copy.wait_recv()
        before = jnp.concatenate([zr[j].astype(f32) for j in range(COL)], axis=0)
        copies = []
        for i in list(range(1, ROW)) + [0]:
            to = row_peer(i)
            s4[to, 0:128] = (before + ebuf[to, 0:128]).astype(bf16)
            if diag is not None:
                s4[to, 128:144] = diag_rows(diag + diag_of(ebuf[to, 128:144]))
            if i:
                copies.append(send(stage, i, s4.at[to], everything.at[me], True))
            else:
                everything[me] = s4[me]
        return copies

    def normalized_queries(heads):
        for h in heads:
            q32 = q[:, h * DH : (h + 1) * DH].astype(f32)
            q_t = (q32 * lax.rsqrt(jnp.sum(q32 * q32, axis=1, keepdims=True) + EPS)).T
            r[h] = q_t
            p[h] = q_t
            rr[h] = jnp.broadcast_to(sums(q_t * q_t), (8, TOK))

    wait_k2 = row_sums(wait_k1, row_k, ebuf_k, cs_k, cr_k, 2, True)
    normalized_queries(range(0, 4))
    wait_v2 = row_sums(wait_v1, row_v, ebuf_v, cs_v, cr_v, 3, False)
    wait_k3 = col_sums(wait_k2, cr_k, zs_k, zr_k, 4)
    normalized_queries(range(4, 8))
    diag = jnp.zeros((1, 128), f32)
    for s in range(COL):
        diag = diag + jnp.where(s < z, diag_of(cr_k[s, 16:32].astype(f32)), 0.0)
    wait_v3 = col_sums(wait_v2, cr_v, zs_v, zr_v, 5)
    for j in range(Y):
        part = slice(1024 * j, 1024 * j + 1024)
        sg[:, part] = gain[:, part] * jax.nn.sigmoid(gate[:, part].astype(f32))
    wait_k4 = hand_out(wait_k3, zr_k, ebuf_k, s4_k, all_k, 6, diag)
    wait_v4 = hand_out(wait_v3, zr_v, ebuf_v, s4_v, all_v, 7, None)

    for copy in wait_k4:
        copy.wait_recv()
    for h in range(HEADS):
        before = all_k[h, 0:128]
        mix[h, :, 0:128] = before
        mix[h, :, 128:256] = before
        mix[h, :, 256:512] = kt[h]
        d = diag_of(all_k[h, 128:144].astype(f32)) + ridge[h : h + 1]
        dgb[h] = jnp.broadcast_to(jnp.sum(jnp.where(eye, d, 0.0), axis=1, keepdims=True), (128, 128))

    def apply(h, direction):
        pp = stack(direction)
        inner = weigh(dot(keys2[h], pp), w[h, 0], w[h, 1], w[h, 2]).astype(bf16)
        d = dgb[h]
        return dot(mix[h], jnp.concatenate([pp, inner], axis=0)) + jnp.concatenate([d, d], axis=1) * direction

    wait_y = []
    for group in range(HEADS // GROUP):
        heads = range(group * GROUP, (group + 1) * GROUP)

        def sweep(step, carry, heads=heads):
            images = [apply(h, p[h]) for h in heads]
            for h, image in zip(heads, images):
                direction, norm_now = p[h], rr[h][0:1]
                alpha = norm_now / sums(direction * image)
                x[h] = jnp.where(step == 0, 0.0, x[h]) + alpha * direction
                residual = r[h] - alpha * image
                r[h] = residual
                norm_next = sums(residual * residual)
                p[h] = residual + (norm_next / norm_now) * direction
                rr[h] = jnp.broadcast_to(norm_next, (8, TOK))
            return carry

        lax.fori_loop(0, ITERS - 1, sweep, 0)
        if group == 0:
            for copy in wait_v4:
                copy.wait_recv()
        for h in heads:
            direction = p[h]
            alpha = rr[h][0:1] / sums(direction * apply(h, direction))
            xx = stack(x[h] + alpha * direction)
            cv = cvb[h]
            top = cv[0:128]
            scores = weigh(dot(keys2[h], xx), jnp.where(tri, top, 0.0), top, jnp.where(tri, cv[128:256], 0.0))
            hi, lo = split(scores)
            before = all_v[h]
            mesa_t = dot(jnp.concatenate([before, before], axis=1), xx) + dot(vt[h], hi) + dot(vt[h], lo)
            mesa[:, h * DH : (h + 1) * DH] = mesa_t.T.astype(bf16)
        cols = slice(group * GROUP * DH, (group + 1) * GROUP * DH)
        for i in range(1, Y):
            to = (y + i) % Y
            copy = pltpu.make_async_remote_copy(
                src_ref=mesa.at[pl.ds(pl.multiple_of(to * ROWS_OUT, ROWS_OUT), ROWS_OUT), cols],
                dst_ref=full.at[y, :, cols],
                send_sem=ysend.at[group, i - 1],
                recv_sem=yrecv.at[group, i - 1],
                device_id=(seq, to),
                device_id_type=MESH,
            )
            copy.start()
            wait_y.append(copy)
    full[y] = mesa[pl.ds(pl.multiple_of(y * ROWS_OUT, ROWS_OUT), ROWS_OUT), :]
    for copy in wait_y:
        copy.wait_recv()
    square = jnp.zeros((ROWS_OUT, 1), f32)
    for j in range(Y):
        part = full[j].astype(f32)
        square = square + jnp.sum(part * part, axis=1, keepdims=True)
    factor = lax.rsqrt(square * (1.0 / (Y * HEADS * DH)) + EPS)
    for j in range(Y):
        cols = slice(1024 * j, 1024 * j + 1024)
        out[:, cols] = (full[j].astype(f32) * factor * sg[:, cols]).astype(bf16)
    for copy in started + wait_y:
        copy.wait_send()


def shards(queries, key_rows, values, write_gate, ridge_diag, norm_gain, gate_logits):
    V = pltpu.VMEM
    D = Y * HEADS * DH

    def comm(rows, piece):
        return [
            V((ROW, rows, 128), bf16),
            V((ROW, rows, 128), bf16),
            V((ROW, rows, 128), f32),
            V((COL, piece, 128), bf16),
            V((COL, piece, 128), bf16),
            V((COL, 16, 128), bf16),
            V((COL, 16, 128), bf16),
            V((ROW, rows, 128), bf16),
            V((ROW, rows, 128), bf16),
        ]

    state = V((HEADS, DH, TOK), f32)
    return pl.pallas_call(
        kernel,
        out_shape=jax.ShapeDtypeStruct((ROWS_OUT, D), bf16),
        in_specs=[pl.BlockSpec(memory_space=pltpu.VMEM)] * 7,
        out_specs=pl.BlockSpec(memory_space=pltpu.VMEM),
        scratch_shapes=[
            V((HEADS, TOK, 2 * DH), bf16),
            V((HEADS, DH, 4 * DH), bf16),
            V((HEADS, DH, TOK), bf16),
            V((HEADS, DH, TOK), bf16),
            V((HEADS, 3, 128, 128), f32),
            V((HEADS, TOK, DH), f32),
            state,
            state,
            state,
            V((HEADS, 8, TOK), f32),
            V((HEADS, DH, DH), f32),
            V((ROWS_OUT, D), f32),
            V((TOK, HEADS * DH), bf16),
            V((Y, ROWS_OUT, HEADS * DH), bf16),
            *comm(144, 32),
            *comm(128, 16),
            pltpu.SemaphoreType.DMA((8, 7)),
            pltpu.SemaphoreType.DMA((8, 7)),
            pltpu.SemaphoreType.DMA((HEADS // GROUP, 3)),
            pltpu.SemaphoreType.DMA((HEADS // GROUP, 3)),
        ],
        compiler_params=pltpu.CompilerParams(
            collective_id=0, has_side_effects=True, vmem_limit_bytes=48 << 20
        ),
    )(queries, key_rows, values, write_gate, ridge_diag, norm_gain.reshape(1, D), gate_logits)


def solution(mesh):
    return jax.shard_map(
        shards,
        mesh=mesh,
        in_specs=(
            P("seq", "head"),
            P("seq", "head"),
            P("seq", "head"),
            P("seq", "head"),
            P("head", None),
            P(),
            P(("seq", "head"), None),
        ),
        out_specs=P(("seq", "head"), None),
        check_vma=False,
    )
```

```python
import functools

import jax
import jax.numpy as jnp
from jax import lax
from jax.experimental import pallas as pl
from jax.experimental.pallas import tpu as pltpu
from jax.sharding import PartitionSpec as P

MESH = pl.DeviceIdType.MESH
f32, bf16 = jnp.float32, jnp.bfloat16
ITERS = 8
HEADS = 8
DH = 128
TOK = 256
ROW = 8
COL = 8
Y = 4
QUARTER = TOK // Y
D = Y * HEADS * DH
EPS = 1e-6
FIRST, LAST = (0, 1), (2, 3, 6, 7, 4, 5)
FINISH = ((0, 1, 2, 3), (6, 7, 4, 5))


def dot(a, b):
    return jnp.dot(a, b, preferred_element_type=f32)


def sums(x):
    return jnp.sum(x, axis=0, keepdims=True)


def split(x):
    hi = x.astype(bf16)
    return hi, (x - hi.astype(f32)).astype(bf16)


def stack(x):
    return jnp.concatenate(split(x), axis=0)


def iota(shape, axis):
    return lax.broadcasted_iota(jnp.int32, shape, axis)


def causal(scores, tri):
    top = jnp.concatenate([jnp.where(tri, scores[0:128, 0:128], 0.0), scores[0:128, 128:256]], axis=1)
    bottom = jnp.concatenate(
        [jnp.zeros((128, 128), f32), jnp.where(tri, scores[128:256, 128:256], 0.0)], axis=1
    )
    return jnp.concatenate([top, bottom], axis=0)


def diag_rows(d):
    hi = d.astype(bf16).astype(f32)
    row = iota((16, 128), 0)
    return jnp.where(row == 0, hi, jnp.where(row == 1, d - hi, 0.0)).astype(bf16)


def diag_of(rows):
    return rows[0:1] + rows[1:2]


def flip(a, s):
    for bit in (1, 2, 4):
        if s & bit:
            a = a + bit - 2 * bit * ((a // bit) % 2)
    return a


def kernel(
    q, k, v, wgt, ridge, gain, gate, out,
    kbuf, qbuf, vbuf, wbuf, rbuf, nbuf, gbuf,
    keys2, mix, gg, vct, r, p, x, rr, cvs, dgb, sg, mesa, full,
    snd_k, row_k, e_k, cs_k, cr_k, zs_k, zr_k, s4_k, all_k,
    snd_v, row_v, e_v, cs_v, cr_v, zs_v, zr_v, s4_v, all_v,
    rs_s, rs_r, cs_s, cs_r, os_s, os_r, loc,
):
    seq, y = lax.axis_index("seq"), lax.axis_index("head")
    z, me = seq // ROW, seq % ROW
    heads = [flip(me, s) for s in range(HEADS)]

    barrier = pltpu.get_barrier_semaphore()
    for i in range(1, ROW):
        pl.semaphore_signal(barrier, inc=1, device_id=(z * ROW + heads[i], y), device_id_type=MESH)
    for i in range(1, COL):
        pl.semaphore_signal(barrier, inc=1, device_id=(flip(z, i) * ROW + me, y), device_id_type=MESH)
    for i in range(1, Y):
        pl.semaphore_signal(barrier, inc=1, device_id=(seq, flip(y, i)), device_id_type=MESH)

    def columns(ref, s):
        return ref.at[:, pl.ds(pl.multiple_of(heads[s] * DH, DH), DH)]

    local = {}

    def fetch(name, src, dst):
        local[name] = pltpu.make_async_copy(src, dst, loc.at[len(local)])
        local[name].start()

    fetch("w", wgt, wbuf)
    for s in ORDER:
        fetch(("k", s), columns(k, s), kbuf.at[s])
    started = []

    def start(src, dst, ssem, rsem, device):
        copy = pltpu.make_async_remote_copy(
            src_ref=src, dst_ref=dst, send_sem=ssem, recv_sem=rsem, device_id=device, device_id_type=MESH
        )
        copy.start()
        started.append(copy)
        return copy

    def to_row(stage, s, src, dst):
        sems = rs_s.at[stage, s - 1], rs_r.at[stage, s - 1]
        return start(src.at[s], dst.at[s], *sems, (z * ROW + heads[s], y))

    def to_col(stage, src, dst):
        return [
            start(
                src.at[flip(z, i)],
                dst.at[z],
                cs_s.at[stage, i - 1],
                cs_r.at[stage, i - 1],
                (flip(z, i) * ROW + me, y),
            )
            for i in range(1, COL)
        ]

    eye = iota((128, 128), 0) == iota((128, 128), 1)
    tri = iota((128, 128), 0) <= iota((128, 128), 1)

    local["w"].wait()
    wait_k1 = []
    for s in ORDER:
        local["k", s].wait()
        kb = kbuf[s]
        k_t = kb.astype(f32).T
        inv = lax.rsqrt(sums(k_t * k_t) + EPS)
        cv = wbuf[pl.ds(heads[s], 1), :] * inv
        kc_t = (k_t * (cv * inv)).astype(bf16)
        state = dot(kc_t, kb)
        snd_k[s, 0:128] = jnp.where(eye, 0.0, state).astype(bf16)
        snd_k[s, 128:144] = diag_rows(sums(jnp.where(eye, state, 0.0)))
        if s == ORDER[0]:
            pl.semaphore_wait(barrier, ROW + COL + Y - 3)
        if s:
            wait_k1.append(to_row(0, s, snd_k, row_k))
            fetch(("v", s), columns(v, s), vbuf.at[s])
        else:
            row_k[0] = snd_k[0]
            fetch(("v", 0), columns(v, 0), vbuf.at[0])
        cvs[s] = jnp.broadcast_to(cv, (8, TOK))
        mix[s, :, 256:512] = kc_t
    for s in range(HEADS):
        fetch(("q", s), columns(q, s), qbuf.at[s])
    fetch("r", ridge, rbuf)
    fetch("n", gain, nbuf)
    fetch("g", gate, gbuf)
    wait_v1 = []
    for s in ORDER:
        local["v", s].wait()
        vc_t = (vbuf[s].astype(f32).T * cvs[s, 0:1]).astype(bf16)
        vct[s] = vc_t
        snd_v[s] = dot(vc_t, kbuf[s]).astype(bf16)
        if s:
            wait_v1.append(to_row(1, s, snd_v, row_v))
        else:
            row_v[0] = snd_v[0]

    def row_sums(waits, rows, e, pieces, landed, stage, with_diag):
        for copy in waits:
            copy.wait_recv()
        total = rows[0].astype(f32)
        for b in range(1, ROW):
            total = total + rows[b].astype(f32)
        tail = diag_rows(diag_of(total[128:144])) if with_diag else None
        for j in range(COL):
            pieces[j, 0:16] = total[16 * j : 16 * j + 16].astype(bf16)
            if with_diag:
                pieces[j, 16:32] = tail
        landed[z] = pieces[z]
        copies = to_col(stage, pieces, landed)
        total = jnp.zeros(e.shape[1:], f32)
        for b in range(ROW):
            e[b] = total
            if b < ROW - 1:
                total = total + rows[flip(me, b)].astype(f32)
        return copies

    def col_sums(waits, landed, zs, zr, stage):
        for copy in waits:
            copy.wait_recv()
        total = jnp.zeros((16, 128), f32)
        for b in range(COL):
            zs[b] = total.astype(bf16)
            total = total + landed[b, 0:16].astype(f32)
        zr[z] = zs[z]
        return to_col(stage, zs, zr)

    def hand_out(waits, zr, e, s4, everything, stage, diag):
        for copy in waits:
            copy.wait_recv()
        before = jnp.concatenate([zr[j].astype(f32) for j in range(COL)], axis=0)
        copies = {}
        for s in (1, 4, 5, 2, 3, 6, 7, 0):
            row = e[heads[s]]
            s4[s, 0:128] = (before + row[0:128]).astype(bf16)
            if diag is not None:
                s4[s, 128:144] = diag_rows(diag + diag_of(row[128:144]))
            if s:
                copies[s] = to_row(stage, s, s4, everything)
            else:
                everything[0] = s4[0]
        return copies

    wait_k2 = row_sums(wait_k1, row_k, e_k, cs_k, cr_k, 0, True)

    for s in range(HEADS):
        local["q", s].wait()
        q_t = qbuf[s].astype(f32).T
        q_t = q_t * lax.rsqrt(sums(q_t * q_t) + EPS)
        r[s] = q_t
        p[s] = q_t
        x[s] = jnp.zeros((DH, TOK), f32)
        rr[s] = jnp.broadcast_to(sums(q_t * q_t), (8, TOK))
        keys2[s, :, 0:128] = kbuf[s]
        keys2[s, :, 128:256] = kbuf[s]
    wait_v2 = row_sums(wait_v1, row_v, e_v, cs_v, cr_v, 1, False)

    wait_k3 = col_sums(wait_k2, cr_k, zs_k, zr_k, 2)
    diag = jnp.zeros((1, 128), f32)
    for b in range(COL):
        diag = diag + jnp.where(b < z, diag_of(cr_k[b, 16:32].astype(f32)), 0.0)
    for name in ("r", "n", "g"):
        local[name].wait()
    for j in range(Y):
        part = slice(1024 * j, 1024 * j + 1024)
        sg[:, part] = nbuf[:, part] * jax.nn.sigmoid(gbuf[:, part].astype(f32))
    wait_v3 = col_sums(wait_v2, cr_v, zs_v, zr_v, 3)
    wait_k4 = hand_out(wait_k3, zr_k, e_k, s4_k, all_k, 2, diag)

    def apply(s, direction):
        pp = stack(direction)
        inner = causal(dot(keys2[s], pp), tri).astype(bf16)
        d = dgb[s]
        return dot(mix[s], jnp.concatenate([pp, inner], axis=0)) + jnp.concatenate([d, d], axis=1) * direction

    def solve(slots):
        for s in slots:
            if s:
                wait_k4[s].wait_recv()
            before = all_k[s, 0:128]
            mix[s, :, 0:128] = before
            mix[s, :, 128:256] = before
            d = diag_of(all_k[s, 128:144].astype(f32)) + rbuf[pl.ds(heads[s], 1), :]
            dgb[s] = jnp.broadcast_to(jnp.sum(jnp.where(eye, d, 0.0), axis=1, keepdims=True), (128, 128))

        def sweep(step, carry):
            images = [apply(s, p[s]) for s in slots]
            for s, image in zip(slots, images):
                direction, norm_now = p[s], rr[s][0:1]
                alpha = norm_now / sums(direction * image)
                x[s] = x[s] + alpha * direction
                residual = r[s] - alpha * image
                r[s] = residual
                norm_next = sums(residual * residual)
                p[s] = residual + (norm_next / norm_now) * direction
                rr[s] = jnp.broadcast_to(norm_next, (8, TOK))
            return carry

        lax.fori_loop(0, ITERS - 1, sweep, 0, unroll=True)

    wait_out = []

    def finish(slots):
        for s in slots:
            if s:
                wait_v4[s].wait_recv()
            gg[s, :, 0:128] = all_v[s]
            gg[s, :, 128:256] = all_v[s]
        images = [apply(s, p[s]) for s in slots]
        found = [stack(x[s] + (rr[s][0:1] / sums(p[s] * image)) * p[s]) for s, image in zip(slots, images)]
        scores = [causal(dot(keys2[s], xx), tri).astype(bf16) for s, xx in zip(slots, found)]
        results = [
            dot(jnp.concatenate([gg[s], vct[s]], axis=1), jnp.concatenate([xx, inner], axis=0))
            for s, xx, inner in zip(slots, found, scores)
        ]
        for s, result in zip(slots, results):
            mesa[s] = result.T.astype(bf16)
        for s in slots:
            for i in range(1, Y):
                to = flip(y, i)
                wait_out.append(
                    start(
                        mesa.at[s, pl.ds(pl.multiple_of(to * QUARTER, QUARTER), QUARTER), :],
                        full.at[y, heads[s]],
                        os_s.at[s, i - 1],
                        os_r.at[s, i - 1],
                        (seq, to),
                    )
                )
            full[y, heads[s]] = mesa[s, pl.ds(pl.multiple_of(y * QUARTER, QUARTER), QUARTER), :]

    solve(FIRST)
    wait_v4 = hand_out(wait_v3, zr_v, e_v, s4_v, all_v, 3, None)
    solve(LAST)
    for slots in FINISH:
        finish(slots)

    for copy in wait_out:
        copy.wait_recv()
    square = jnp.zeros((QUARTER, DH), f32)
    for j in range(Y):
        for h in range(HEADS):
            part = full[j, h].astype(f32)
            square = square + part * part
    factor = lax.rsqrt(jnp.sum(square, axis=1, keepdims=True) * (1.0 / D) + EPS)
    for j in range(Y):
        for h in range(HEADS):
            cols = slice((j * HEADS + h) * DH, (j * HEADS + h + 1) * DH)
            out[:, cols] = (full[j, h].astype(f32) * factor * sg[:, cols]).astype(bf16)
    for copy in started:
        copy.wait_send()


ORDER = (4, 5, 2, 3, 6, 7, 1, 0)


def shards(queries, key_rows, values, write_gate, ridge_diag, norm_gain, gate_logits):
    V = pltpu.VMEM
    raw = V((HEADS, TOK, DH), bf16)
    state = V((HEADS, DH, TOK), f32)
    col = V((COL, 16, DH), bf16)
    wide = V((COL, 32, DH), bf16)

    def comm(rows, piece):
        sent = V((ROW, rows, DH), bf16)
        return sent, sent, V((ROW, rows, DH), f32), piece, piece, col, col, sent, sent

    hbm, vmem = pl.BlockSpec(memory_space=pltpu.HBM), pl.BlockSpec(memory_space=pltpu.VMEM)
    return pl.pallas_call(
        kernel,
        out_shape=jax.ShapeDtypeStruct((QUARTER, D), bf16),
        in_specs=[hbm] * 7,
        out_specs=vmem,
        scratch_shapes=[
            raw,
            raw,
            raw,
            V((HEADS, TOK), f32),
            V((HEADS, DH), f32),
            V((1, D), f32),
            V((QUARTER, D), bf16),
            V((HEADS, TOK, 2 * DH), bf16),
            V((HEADS, DH, 4 * DH), bf16),
            V((HEADS, DH, 2 * DH), bf16),
            V((HEADS, DH, TOK), bf16),
            state,
            state,
            state,
            V((HEADS, 8, TOK), f32),
            V((HEADS, 8, TOK), f32),
            V((HEADS, DH, DH), f32),
            V((QUARTER, D), f32),
            raw,
            V((Y, HEADS, QUARTER, DH), bf16),
            *comm(144, wide),
            *comm(128, col),
            pltpu.SemaphoreType.DMA((4, 7)),
            pltpu.SemaphoreType.DMA((4, 7)),
            pltpu.SemaphoreType.DMA((4, 7)),
            pltpu.SemaphoreType.DMA((4, 7)),
            pltpu.SemaphoreType.DMA((HEADS, Y - 1)),
            pltpu.SemaphoreType.DMA((HEADS, Y - 1)),
            pltpu.SemaphoreType.DMA((28,)),
        ],
        compiler_params=pltpu.CompilerParams(
            collective_id=0, has_side_effects=True, vmem_limit_bytes=56 << 20
        ),
    )(queries, key_rows, values, write_gate.T, ridge_diag, norm_gain.reshape(1, D), gate_logits)


def solution(mesh):
    return jax.shard_map(
        shards,
        mesh=mesh,
        in_specs=(
            P("seq", "head"),
            P("seq", "head"),
            P("seq", "head"),
            P("seq", "head"),
            P("head", None),
            P(),
            P(("seq", "head"), None),
        ),
        out_specs=P(("seq", "head"), None),
        check_vma=False,
    )
```

```python
import functools

import jax
import jax.numpy as jnp
from jax import lax
from jax.experimental import pallas as pl
from jax.experimental.pallas import tpu as pltpu
from jax.sharding import PartitionSpec as P

MESH = pl.DeviceIdType.MESH
f32, bf16 = jnp.float32, jnp.bfloat16
ITERS = 8
HEADS = 8
DH = 128
TOK = 256
ROW = 8
COL = 8
Y = 4
QUARTER = TOK // Y
D = Y * HEADS * DH
EPS = 1e-6
FIRST, LAST = (0, 1), (2, 3, 6, 7, 4, 5)
FINISH = ((2, 3, 6), (7, 4, 5))


def dot(a, b):
    return jnp.dot(a, b, preferred_element_type=f32)


def sums(x):
    return jnp.sum(x, axis=0, keepdims=True)


def split(x):
    hi = x.astype(bf16)
    return hi, (x - hi.astype(f32)).astype(bf16)


def stack(x):
    return jnp.concatenate(split(x), axis=0)


def iota(shape, axis):
    return lax.broadcasted_iota(jnp.int32, shape, axis)


def causal(scores, tri):
    top = jnp.concatenate([jnp.where(tri, scores[0:128, 0:128], 0.0), scores[0:128, 128:256]], axis=1)
    bottom = jnp.concatenate(
        [jnp.zeros((128, 128), f32), jnp.where(tri, scores[128:256, 128:256], 0.0)], axis=1
    )
    return jnp.concatenate([top, bottom], axis=0)


def diag_rows(d):
    hi = d.astype(bf16).astype(f32)
    row = iota((16, 128), 0)
    return jnp.where(row == 0, hi, jnp.where(row == 1, d - hi, 0.0)).astype(bf16)


def diag_of(rows):
    return rows[0:1] + rows[1:2]


def flip(a, s):
    for bit in (1, 2, 4):
        if s & bit:
            a = a + bit - 2 * bit * ((a // bit) % 2)
    return a


def pack(state):
    row, lane = iota((64, 128), 0), iota((64, 128), 1)
    low = pltpu.roll(state[64:128], 64, 1)
    return jnp.where(lane > row, state[0:64], jnp.where(lane < row, low, 0.0))


def unpack(half):
    row, lane = iota((64, 128), 0), iota((64, 128), 1)
    low = pltpu.roll(jnp.where(lane < row, half, 0.0), 64, 1)
    upper = jnp.concatenate([jnp.where(lane > row, half, 0.0), low], axis=0)
    return upper + upper.T


def kernel(
    q, k, v, wgt, ridge, gain, gate, out,
    kbuf, qbuf, vbuf, wbuf, rbuf, nbuf, gbuf,
    keys2, mix, gg, vct, r, p, x, rr, cvs, dgb, sg, mesa, full,
    snd_k, row_k, e_k, cs_k, cr_k, zs_k, zr_k, s4_k, all_k,
    snd_v, row_v, e_v, cs_v, cr_v, zs_v, zr_v, s4_v, all_v,
    rs_s, rs_r, cs_s, cs_r, os_s, os_r, loc,
):
    seq, y = lax.axis_index("seq"), lax.axis_index("head")
    z, me = seq // ROW, seq % ROW
    heads = [flip(me, s) for s in range(HEADS)]

    barrier = pltpu.get_barrier_semaphore()
    for i in range(1, ROW):
        pl.semaphore_signal(barrier, inc=1, device_id=(z * ROW + heads[i], y), device_id_type=MESH)
    for i in range(1, COL):
        pl.semaphore_signal(barrier, inc=1, device_id=(flip(z, i) * ROW + me, y), device_id_type=MESH)
    for i in range(1, Y):
        pl.semaphore_signal(barrier, inc=1, device_id=(seq, flip(y, i)), device_id_type=MESH)

    def columns(ref, s):
        return ref.at[:, pl.ds(pl.multiple_of(heads[s] * DH, DH), DH)]

    local = {}

    def fetch(name, src, dst):
        local[name] = pltpu.make_async_copy(src, dst, loc.at[len(local)])
        local[name].start()

    fetch("w", wgt, wbuf)
    for s in ORDER:
        fetch(("k", s), columns(k, s), kbuf.at[s])
    started = []

    def start(src, dst, ssem, rsem, device):
        copy = pltpu.make_async_remote_copy(
            src_ref=src, dst_ref=dst, send_sem=ssem, recv_sem=rsem, device_id=device, device_id_type=MESH
        )
        copy.start()
        started.append(copy)
        return copy

    def to_row(stage, s, src, dst):
        sems = rs_s.at[stage, s - 1], rs_r.at[stage, s - 1]
        return start(src.at[s], dst.at[s], *sems, (z * ROW + heads[s], y))

    def to_col(stage, src, dst):
        return [
            start(
                src.at[flip(z, i)],
                dst.at[z],
                cs_s.at[stage, i - 1],
                cs_r.at[stage, i - 1],
                (flip(z, i) * ROW + me, y),
            )
            for i in range(1, COL)
        ]

    eye = iota((128, 128), 0) == iota((128, 128), 1)
    tri = iota((128, 128), 0) <= iota((128, 128), 1)

    local["w"].wait()
    wait_k1 = []
    for batch in (ORDER[:4], ORDER[4:]):
        for s in batch:
            local["k", s].wait()
        keys_t = [kbuf[s].astype(f32).T for s in batch]
        invs = [lax.rsqrt(sums(k_t * k_t) + EPS) for k_t in keys_t]
        gates = [wbuf[pl.ds(heads[s], 1), :] * inv for s, inv in zip(batch, invs)]
        weighed = [(k_t * (cv * inv)).astype(bf16) for k_t, cv, inv in zip(keys_t, gates, invs)]
        states = [dot(kc_t, kbuf[s]) for s, kc_t in zip(batch, weighed)]
        for s, state in zip(batch, states):
            snd_k[s, 0:64] = pack(state).astype(bf16)
            snd_k[s, 64:80] = diag_rows(sums(jnp.where(eye, state, 0.0)))
        for s, cv, kc_t in zip(batch, gates, weighed):
            cvs[s] = jnp.broadcast_to(cv, (8, TOK))
            mix[s, :, 256:512] = kc_t
        if batch[0] == ORDER[0]:
            pl.semaphore_wait(barrier, ROW + COL + Y - 3)
        for s in batch:
            if s:
                wait_k1.append(to_row(0, s, snd_k, row_k))
        for s in batch:
            fetch(("v", s), columns(v, s), vbuf.at[s])
    row_k[0] = snd_k[0]
    for s in range(HEADS):
        fetch(("q", s), columns(q, s), qbuf.at[s])
    fetch("r", ridge, rbuf)
    fetch("n", gain, nbuf)
    fetch("g", gate, gbuf)
    wait_v1 = []
    for batch in (ORDER[:4], ORDER[4:]):
        for s in batch:
            local["v", s].wait()
        weighed = [(vbuf[s].astype(f32).T * cvs[s, 0:1]).astype(bf16) for s in batch]
        states = [dot(vc_t, kbuf[s]) for s, vc_t in zip(batch, weighed)]
        for s, vc_t, state in zip(batch, weighed, states):
            vct[s] = vc_t
            snd_v[s] = state.astype(bf16)
        for s in batch:
            if s:
                wait_v1.append(to_row(1, s, snd_v, row_v))
    row_v[0] = snd_v[0]

    def row_sums(waits, rows, e, pieces, landed, stage, with_diag):
        for copy in waits:
            copy.wait_recv()
        total = rows[0].astype(f32)
        for b in range(1, ROW):
            total = total + rows[b].astype(f32)
        for j in range(COL):
            if with_diag:
                pieces[j, 0:8] = total[8 * j : 8 * j + 8]
                pieces[j, 8:16] = jnp.broadcast_to(diag_of(total[64:80]), (8, 128))
            else:
                pieces[j] = total[16 * j : 16 * j + 16].astype(bf16)
        landed[z] = pieces[z]
        copies = to_col(stage, pieces, landed)
        total = jnp.zeros(e.shape[1:], f32)
        for b in range(ROW):
            e[b] = total
            if b < ROW - 1:
                total = total + rows[flip(me, b)].astype(f32)
        return copies

    def col_sums(waits, landed, zs, zr, stage):
        for copy in waits:
            copy.wait_recv()
        rows = zs.shape[1]
        total = jnp.zeros((rows, 128), f32)
        for b in range(COL):
            zs[b] = total.astype(zs.dtype)
            total = total + landed[b, 0:rows].astype(f32)
        zr[z] = zs[z]
        return to_col(stage, zs, zr)

    def hand_out(waits, zr, e, s4, everything, stage, diag):
        for copy in waits:
            copy.wait_recv()
        before = jnp.concatenate([zr[j].astype(f32) for j in range(COL)], axis=0)
        copies = {}
        for batch in ((1, 4, 5, 2), (3, 6, 7, 0)):
            for s in batch:
                row = e[heads[s]]
                rows = before.shape[0]
                s4[s, 0:rows] = (before + row[0:rows]).astype(bf16)
                if diag is not None:
                    s4[s, 64:80] = diag_rows(diag + diag_of(row[64:80]))
            for s in batch:
                if s:
                    copies[s] = to_row(stage, s, s4, everything)
        everything[0] = s4[0]
        return copies

    wait_k2 = row_sums(wait_k1, row_k, e_k, cs_k, cr_k, 0, True)
    wait_v2 = row_sums(wait_v1, row_v, e_v, cs_v, cr_v, 1, False)

    for s in range(HEADS):
        local["q", s].wait()
        q_t = qbuf[s].astype(f32).T
        q_t = q_t * lax.rsqrt(sums(q_t * q_t) + EPS)
        r[s] = q_t
        p[s] = q_t
        x[s] = jnp.zeros((DH, TOK), f32)
        rr[s] = jnp.broadcast_to(sums(q_t * q_t), (8, TOK))
        keys2[s, :, 0:128] = kbuf[s]
        keys2[s, :, 128:256] = kbuf[s]
    wait_k3 = col_sums(wait_k2, cr_k, zs_k, zr_k, 2)
    wait_v3 = col_sums(wait_v2, cr_v, zs_v, zr_v, 3)
    diag = jnp.zeros((1, 128), f32)
    for b in range(COL):
        diag = diag + jnp.where(b < z, cr_k[b, 8:9], 0.0)
    for name in ("r", "n", "g"):
        local[name].wait()
    for j in range(Y):
        part = slice(1024 * j, 1024 * j + 1024)
        sg[:, part] = nbuf[:, part] * jax.nn.sigmoid(gbuf[:, part].astype(f32))
    wait_k4 = hand_out(wait_k3, zr_k, e_k, s4_k, all_k, 2, diag)

    def apply(s, direction):
        pp = stack(direction)
        inner = causal(dot(keys2[s], pp), tri).astype(bf16)
        d = dgb[s]
        return dot(mix[s], jnp.concatenate([pp, inner], axis=0)) + jnp.concatenate([d, d], axis=1) * direction

    def place_states(slots):
        for s in slots:
            if s:
                wait_k4[s].wait_recv()
            before = unpack(all_k[s, 0:64].astype(f32)).astype(bf16)
            mix[s, :, 0:128] = before
            mix[s, :, 128:256] = before
            d = diag_of(all_k[s, 64:80].astype(f32)) + rbuf[pl.ds(heads[s], 1), :]
            dgb[s] = jnp.broadcast_to(jnp.sum(jnp.where(eye, d, 0.0), axis=1, keepdims=True), (128, 128))

    def sweep(slots):
        images = [apply(s, p[s]) for s in slots]
        for s, image in zip(slots, images):
            direction, norm_now = p[s], rr[s][0:1]
            alpha = norm_now / sums(direction * image)
            x[s] = x[s] + alpha * direction
            residual = r[s] - alpha * image
            r[s] = residual
            norm_next = sums(residual * residual)
            p[s] = residual + (norm_next / norm_now) * direction
            rr[s] = jnp.broadcast_to(norm_next, (8, TOK))

    def sweeps(slots, count):
        def step(n, carry):
            sweep(slots)
            return carry

        lax.fori_loop(0, count, step, 0, unroll=True)

    wait_out = []

    def solution_of(slots):
        images = [apply(s, p[s]) for s in slots]
        return [stack(x[s] + (rr[s][0:1] / sums(p[s] * image)) * p[s]) for s, image in zip(slots, images)]

    def attention(slots, found):
        return [causal(dot(keys2[s], xx), tri).astype(bf16) for s, xx in zip(slots, found)]

    def place_values(slots):
        for s in slots:
            if s:
                wait_v4[s].wait_recv()
            gg[s, :, 0:128] = all_v[s]
            gg[s, :, 128:256] = all_v[s]

    def results(slots, found, inner):
        outs = [
            dot(jnp.concatenate([gg[s], vct[s]], axis=1), jnp.concatenate([xx, scores], axis=0))
            for s, xx, scores in zip(slots, found, inner)
        ]
        for s, result in zip(slots, outs):
            mesa[s] = result.T.astype(bf16)

    def send_out(slots):
        for s in slots:
            for i in range(1, Y):
                to = flip(y, i)
                wait_out.append(
                    start(
                        mesa.at[s, pl.ds(pl.multiple_of(to * QUARTER, QUARTER), QUARTER), :],
                        full.at[y, heads[s]],
                        os_s.at[s, i - 1],
                        os_r.at[s, i - 1],
                        (seq, to),
                    )
                )
            full[y, heads[s]] = mesa[s, pl.ds(pl.multiple_of(y * QUARTER, QUARTER), QUARTER), :]

    wait_v4 = hand_out(wait_v3, zr_v, e_v, s4_v, all_v, 3, None)
    place_states(FIRST)
    sweeps(FIRST, ITERS - 1)
    place_states(LAST)
    found = solution_of(FIRST)
    sweep(LAST)
    inner = attention(FIRST, found)
    sweep(LAST)
    place_values(FIRST)
    results(FIRST, found, inner)
    sweep(LAST)
    send_out(FIRST)
    sweeps(LAST, ITERS - 4)
    place_values(LAST)
    for slots in FINISH:
        found = solution_of(slots)
        results(slots, found, attention(slots, found))
        send_out(slots)

    for copy in wait_out:
        copy.wait_recv()
    square = jnp.zeros((QUARTER, DH), f32)
    for j in range(Y):
        for h in range(HEADS):
            part = full[j, h].astype(f32)
            square = square + part * part
    factor = lax.rsqrt(jnp.sum(square, axis=1, keepdims=True) * (1.0 / D) + EPS)
    for j in range(Y):
        for h in range(HEADS):
            cols = slice((j * HEADS + h) * DH, (j * HEADS + h + 1) * DH)
            out[:, cols] = (full[j, h].astype(f32) * factor * sg[:, cols]).astype(bf16)
    for copy in started:
        copy.wait_send()


ORDER = (4, 5, 2, 3, 6, 7, 1, 0)


def shards(queries, key_rows, values, write_gate, ridge_diag, norm_gain, gate_logits):
    V = pltpu.VMEM
    raw = V((HEADS, TOK, DH), bf16)
    state = V((HEADS, DH, TOK), f32)
    col = V((COL, 16, DH), bf16)

    def comm(rows, piece, back):
        sent = V((ROW, rows, DH), bf16)
        return sent, sent, V((ROW, rows, DH), f32), piece, piece, back, back, sent, sent

    hbm, vmem = pl.BlockSpec(memory_space=pltpu.HBM), pl.BlockSpec(memory_space=pltpu.VMEM)
    return pl.pallas_call(
        kernel,
        out_shape=jax.ShapeDtypeStruct((QUARTER, D), bf16),
        in_specs=[hbm] * 7,
        out_specs=vmem,
        scratch_shapes=[
            raw,
            raw,
            raw,
            V((HEADS, TOK), f32),
            V((HEADS, DH), f32),
            V((1, D), f32),
            V((QUARTER, D), bf16),
            V((HEADS, TOK, 2 * DH), bf16),
            V((HEADS, DH, 4 * DH), bf16),
            V((HEADS, DH, 2 * DH), bf16),
            V((HEADS, DH, TOK), bf16),
            state,
            state,
            state,
            V((HEADS, 8, TOK), f32),
            V((HEADS, 8, TOK), f32),
            V((HEADS, DH, DH), f32),
            V((QUARTER, D), f32),
            raw,
            V((Y, HEADS, QUARTER, DH), bf16),
            *comm(80, V((COL, 16, DH), f32), V((COL, 8, DH), f32)),
            *comm(128, col, col),
            pltpu.SemaphoreType.DMA((4, 7)),
            pltpu.SemaphoreType.DMA((4, 7)),
            pltpu.SemaphoreType.DMA((4, 7)),
            pltpu.SemaphoreType.DMA((4, 7)),
            pltpu.SemaphoreType.DMA((HEADS, Y - 1)),
            pltpu.SemaphoreType.DMA((HEADS, Y - 1)),
            pltpu.SemaphoreType.DMA((28,)),
        ],
        compiler_params=pltpu.CompilerParams(
            collective_id=0, has_side_effects=True, vmem_limit_bytes=56 << 20
        ),
    )(queries, key_rows, values, write_gate.T, ridge_diag, norm_gain.reshape(1, D), gate_logits)


def solution(mesh):
    return jax.shard_map(
        shards,
        mesh=mesh,
        in_specs=(
            P("seq", "head"),
            P("seq", "head"),
            P("seq", "head"),
            P("seq", "head"),
            P("head", None),
            P(),
            P(("seq", "head"), None),
        ),
        out_specs=P(("seq", "head"), None),
        check_vma=False,
    )
```

```python
import functools

import jax
import jax.numpy as jnp
from jax import lax
from jax.experimental import pallas as pl
from jax.experimental.pallas import tpu as pltpu
from jax.sharding import PartitionSpec as P

MESH = pl.DeviceIdType.MESH
f32, bf16 = jnp.float32, jnp.bfloat16
ITERS = 8
HEADS = 8
DH = 128
TOK = 256
ROW = 8
COL = 8
Y = 4
QUARTER = TOK // Y
D = Y * HEADS * DH
EPS = 1e-6
FIRST, LAST = (0, 1), (2, 3, 6, 7, 4, 5)
FINISH = ((2, 3), (6, 7), (4, 5))


def dot(a, b):
    return jnp.dot(a, b, preferred_element_type=f32)


def sums(x):
    return jnp.sum(x, axis=0, keepdims=True)


def split(x):
    hi = x.astype(bf16)
    return hi, (x - hi.astype(f32)).astype(bf16)


def stack(x):
    return jnp.concatenate(split(x), axis=0)


def iota(shape, axis):
    return lax.broadcasted_iota(jnp.int32, shape, axis)


def causal(scores, tri):
    top = jnp.concatenate([jnp.where(tri, scores[0:128, 0:128], 0.0), scores[0:128, 128:256]], axis=1)
    bottom = jnp.concatenate(
        [jnp.zeros((128, 128), f32), jnp.where(tri, scores[128:256, 128:256], 0.0)], axis=1
    )
    return jnp.concatenate([top, bottom], axis=0)


def diag_rows(d):
    hi = d.astype(bf16).astype(f32)
    row = iota((16, 128), 0)
    return jnp.where(row == 0, hi, jnp.where(row == 1, d - hi, 0.0)).astype(bf16)


def diag_of(rows):
    return rows[0:1] + rows[1:2]


def flip(a, s):
    for bit in (1, 2, 4):
        if s & bit:
            a = a + bit - 2 * bit * ((a // bit) % 2)
    return a


def pack(state):
    row, lane = iota((64, 128), 0), iota((64, 128), 1)
    low = pltpu.roll(state[64:128], 64, 1)
    return jnp.where(lane > row, state[0:64], jnp.where(lane < row, low, 0.0))


def unpack(half):
    row, lane = iota((64, 128), 0), iota((64, 128), 1)
    low = pltpu.roll(jnp.where(lane < row, half, 0.0), 64, 1)
    upper = jnp.concatenate([jnp.where(lane > row, half, 0.0), low], axis=0)
    return upper + upper.T


def kernel(
    q, k, v, wgt, ridge, gain, gate, out,
    kbuf, qbuf, vbuf, wbuf, rbuf, nbuf, gbuf,
    keys2, mix, gg, vct, r, p, x, rr, cvs, dgb, sg, mesa, full,
    snd_k, row_k, e_k, cs_k, cr_k, zs_k, zr_k, s4_k, all_k,
    snd_v, row_v, e_v, cs_v, cr_v, zs_v, zr_v, s4_v, all_v,
    rs_s, rs_r, cs_s, cs_r, os_s, os_r, loc,
):
    seq, y = lax.axis_index("seq"), lax.axis_index("head")
    z, me = seq // ROW, seq % ROW
    heads = [flip(me, s) for s in range(HEADS)]

    barrier = pltpu.get_barrier_semaphore()
    for i in range(1, ROW):
        pl.semaphore_signal(barrier, inc=1, device_id=(z * ROW + heads[i], y), device_id_type=MESH)
    for i in range(1, COL):
        pl.semaphore_signal(barrier, inc=1, device_id=(flip(z, i) * ROW + me, y), device_id_type=MESH)
    for i in range(1, Y):
        pl.semaphore_signal(barrier, inc=1, device_id=(seq, flip(y, i)), device_id_type=MESH)

    def columns(ref, s):
        return ref.at[:, pl.ds(pl.multiple_of(heads[s] * DH, DH), DH)]

    local = {}

    def fetch(name, src, dst):
        local[name] = pltpu.make_async_copy(src, dst, loc.at[len(local)])
        local[name].start()

    fetch("w", wgt, wbuf)
    for s in ORDER:
        fetch(("k", s), columns(k, s), kbuf.at[s])
    started = []

    def start(src, dst, ssem, rsem, device):
        copy = pltpu.make_async_remote_copy(
            src_ref=src, dst_ref=dst, send_sem=ssem, recv_sem=rsem, device_id=device, device_id_type=MESH
        )
        copy.start()
        started.append(copy)
        return copy

    def to_row(stage, s, src, dst):
        sems = rs_s.at[stage, s - 1], rs_r.at[stage, s - 1]
        return start(src.at[s], dst.at[s], *sems, (z * ROW + heads[s], y))

    def to_col(stage, src, dst):
        return [
            start(
                src.at[flip(z, i)],
                dst.at[z],
                cs_s.at[stage, i - 1],
                cs_r.at[stage, i - 1],
                (flip(z, i) * ROW + me, y),
            )
            for i in range(1, COL)
        ]

    eye = iota((128, 128), 0) == iota((128, 128), 1)
    tri = iota((128, 128), 0) <= iota((128, 128), 1)

    local["w"].wait()
    wait_k1 = []
    for batch in (ORDER[:4], ORDER[4:]):
        for s in batch:
            local["k", s].wait()
        keys_t = [kbuf[s].astype(f32).T for s in batch]
        invs = [lax.rsqrt(sums(k_t * k_t) + EPS) for k_t in keys_t]
        gates = [wbuf[pl.ds(heads[s], 1), :] * inv for s, inv in zip(batch, invs)]
        weighed = [(k_t * (cv * inv)).astype(bf16) for k_t, cv, inv in zip(keys_t, gates, invs)]
        states = [dot(kc_t, kbuf[s]) for s, kc_t in zip(batch, weighed)]
        for s, state in zip(batch, states):
            snd_k[s, 0:64] = pack(state).astype(bf16)
            snd_k[s, 64:80] = diag_rows(sums(jnp.where(eye, state, 0.0)))
        for s, cv, kc_t in zip(batch, gates, weighed):
            cvs[s] = jnp.broadcast_to(cv, (8, TOK))
            mix[s, :, 256:512] = kc_t
        if batch[0] == ORDER[0]:
            pl.semaphore_wait(barrier, ROW + COL + Y - 3)
        for s in batch:
            if s:
                wait_k1.append(to_row(0, s, snd_k, row_k))
        for s in batch:
            fetch(("v", s), columns(v, s), vbuf.at[s])
    row_k[0] = snd_k[0]
    for s in range(HEADS):
        fetch(("q", s), columns(q, s), qbuf.at[s])
    fetch("r", ridge, rbuf)
    fetch("n", gain, nbuf)
    fetch("g", gate, gbuf)
    wait_v1 = []
    for batch in (ORDER[:4], ORDER[4:]):
        for s in batch:
            local["v", s].wait()
        weighed = [(vbuf[s].astype(f32).T * cvs[s, 0:1]).astype(bf16) for s in batch]
        states = [dot(vc_t, kbuf[s]) for s, vc_t in zip(batch, weighed)]
        for s, vc_t, state in zip(batch, weighed, states):
            vct[s] = vc_t
            snd_v[s] = state.astype(bf16)
        for s in batch:
            if s:
                wait_v1.append(to_row(1, s, snd_v, row_v))
    row_v[0] = snd_v[0]

    def row_sums(waits, rows, e, pieces, landed, stage, with_diag):
        for copy in waits:
            copy.wait_recv()
        total = rows[0].astype(f32)
        for b in range(1, ROW):
            total = total + rows[b].astype(f32)
        for j in range(COL):
            if with_diag:
                pieces[j, 0:8] = total[8 * j : 8 * j + 8]
                pieces[j, 8:16] = jnp.broadcast_to(diag_of(total[64:80]), (8, 128))
            else:
                pieces[j] = total[16 * j : 16 * j + 16].astype(bf16)
        landed[z] = pieces[z]
        copies = to_col(stage, pieces, landed)
        total = jnp.zeros(e.shape[1:], f32)
        for b in range(ROW):
            e[b] = total
            if b < ROW - 1:
                total = total + rows[flip(me, b)].astype(f32)
        return copies

    def col_sums(waits, landed, zs, zr, stage):
        for copy in waits:
            copy.wait_recv()
        rows = zs.shape[1]
        total = jnp.zeros((rows, 128), f32)
        for b in range(COL):
            zs[b] = total.astype(zs.dtype)
            total = total + landed[b, 0:rows].astype(f32)
        zr[z] = zs[z]
        return to_col(stage, zs, zr)

    def hand_out(waits, zr, e, s4, everything, stage, diag):
        for copy in waits:
            copy.wait_recv()
        before = jnp.concatenate([zr[j].astype(f32) for j in range(COL)], axis=0)
        copies = {}
        for batch in ((1, 4, 5, 2), (3, 6, 7, 0)):
            for s in batch:
                row = e[heads[s]]
                rows = before.shape[0]
                s4[s, 0:rows] = (before + row[0:rows]).astype(bf16)
                if diag is not None:
                    s4[s, 64:80] = diag_rows(diag + diag_of(row[64:80]))
            for s in batch:
                if s:
                    copies[s] = to_row(stage, s, s4, everything)
        everything[0] = s4[0]
        return copies

    wait_k2 = row_sums(wait_k1, row_k, e_k, cs_k, cr_k, 0, True)
    wait_v2 = row_sums(wait_v1, row_v, e_v, cs_v, cr_v, 1, False)

    for s in range(HEADS):
        local["q", s].wait()
        q_t = qbuf[s].astype(f32).T
        q_t = q_t * lax.rsqrt(sums(q_t * q_t) + EPS)
        r[s] = q_t
        p[s] = q_t
        x[s] = jnp.zeros((DH, TOK), f32)
        rr[s] = jnp.broadcast_to(sums(q_t * q_t), (8, TOK))
        keys2[s, :, 0:128] = kbuf[s]
        keys2[s, :, 128:256] = kbuf[s]
    wait_k3 = col_sums(wait_k2, cr_k, zs_k, zr_k, 2)
    wait_v3 = col_sums(wait_v2, cr_v, zs_v, zr_v, 3)
    diag = jnp.zeros((1, 128), f32)
    for b in range(COL):
        diag = diag + jnp.where(b < z, cr_k[b, 8:9], 0.0)
    for name in ("r", "n", "g"):
        local[name].wait()
    for j in range(Y):
        part = slice(1024 * j, 1024 * j + 1024)
        sg[:, part] = nbuf[:, part] * jax.nn.sigmoid(gbuf[:, part].astype(f32))
    wait_k4 = hand_out(wait_k3, zr_k, e_k, s4_k, all_k, 2, diag)

    def apply(s, direction):
        pp = stack(direction)
        inner = causal(dot(keys2[s], pp), tri).astype(bf16)
        d = dgb[s]
        return dot(mix[s], jnp.concatenate([pp, inner], axis=0)) + jnp.concatenate([d, d], axis=1) * direction

    def place_states(slots):
        for s in slots:
            if s:
                wait_k4[s].wait_recv()
        for s in slots:
            before = unpack(all_k[s, 0:64].astype(f32)).astype(bf16)
            mix[s, :, 0:128] = before
            mix[s, :, 128:256] = before
            d = diag_of(all_k[s, 64:80].astype(f32)) + rbuf[pl.ds(heads[s], 1), :]
            dgb[s] = jnp.broadcast_to(jnp.sum(jnp.where(eye, d, 0.0), axis=1, keepdims=True), (128, 128))

    def sweep(slots):
        images = [apply(s, p[s]) for s in slots]
        for s, image in zip(slots, images):
            direction, norm_now = p[s], rr[s][0:1]
            alpha = norm_now / sums(direction * image)
            x[s] = x[s] + alpha * direction
            residual = r[s] - alpha * image
            r[s] = residual
            norm_next = sums(residual * residual)
            p[s] = residual + (norm_next / norm_now) * direction
            rr[s] = jnp.broadcast_to(norm_next, (8, TOK))

    def sweeps(slots, count):
        def step(n, carry):
            sweep(slots)
            return carry

        lax.fori_loop(0, count, step, 0, unroll=True)

    wait_out = []

    def solution_of(slots):
        images = [apply(s, p[s]) for s in slots]
        return [stack(x[s] + (rr[s][0:1] / sums(p[s] * image)) * p[s]) for s, image in zip(slots, images)]

    def attention(slots, found):
        return [causal(dot(keys2[s], xx), tri).astype(bf16) for s, xx in zip(slots, found)]

    def place_values(slots):
        for s in slots:
            if s:
                wait_v4[s].wait_recv()
            gg[s, :, 0:128] = all_v[s]
            gg[s, :, 128:256] = all_v[s]

    def results(slots, found, inner):
        outs = [
            dot(jnp.concatenate([gg[s], vct[s]], axis=1), jnp.concatenate([xx, scores], axis=0))
            for s, xx, scores in zip(slots, found, inner)
        ]
        for s, result in zip(slots, outs):
            mesa[s] = result.T.astype(bf16)

    def send_out(slots):
        for s in slots:
            for i in (2, 1, 3):
                to = flip(y, i)
                wait_out.append(
                    start(
                        mesa.at[s, pl.ds(pl.multiple_of(to * QUARTER, QUARTER), QUARTER), :],
                        full.at[y, heads[s]],
                        os_s.at[s, i - 1],
                        os_r.at[s, i - 1],
                        (seq, to),
                    )
                )
            full[y, heads[s]] = mesa[s, pl.ds(pl.multiple_of(y * QUARTER, QUARTER), QUARTER), :]

    wait_v4 = hand_out(wait_v3, zr_v, e_v, s4_v, all_v, 3, None)
    place_states(FIRST)
    sweeps(FIRST, ITERS - 3)
    place_states(LAST)
    sweep(FIRST + LAST)
    sweep(FIRST + LAST)
    found = solution_of(FIRST)
    sweep(LAST)
    inner = attention(FIRST, found)
    sweep(LAST)
    place_values(FIRST)
    results(FIRST, found, inner)
    sweep(LAST)
    send_out(FIRST)
    sweeps(LAST, ITERS - 6)
    place_values(LAST)
    for slots in FINISH:
        found = solution_of(slots)
        results(slots, found, attention(slots, found))
        send_out(slots)

    square = jnp.zeros((QUARTER, DH), f32)
    for slots in (FIRST, *FINISH):
        for copy in wait_out[: 3 * len(slots)]:
            copy.wait_recv()
        del wait_out[: 3 * len(slots)]
        for s in slots:
            for i in range(Y):
                part = full[flip(y, i), heads[s]].astype(f32)
                square = square + part * part
    factor = lax.rsqrt(jnp.sum(square, axis=1, keepdims=True) * (1.0 / D) + EPS)
    for j in range(Y):
        for h in range(HEADS):
            cols = slice((j * HEADS + h) * DH, (j * HEADS + h + 1) * DH)
            out[:, cols] = (full[j, h].astype(f32) * factor * sg[:, cols]).astype(bf16)
    for copy in started:
        copy.wait_send()


ORDER = (4, 5, 2, 3, 6, 7, 1, 0)


def shards(queries, key_rows, values, write_gate, ridge_diag, norm_gain, gate_logits):
    V = pltpu.VMEM
    raw = V((HEADS, TOK, DH), bf16)
    state = V((HEADS, DH, TOK), f32)
    col = V((COL, 16, DH), bf16)

    def comm(rows, piece, back):
        sent = V((ROW, rows, DH), bf16)
        return sent, sent, V((ROW, rows, DH), f32), piece, piece, back, back, sent, sent

    hbm, vmem = pl.BlockSpec(memory_space=pltpu.HBM), pl.BlockSpec(memory_space=pltpu.VMEM)
    return pl.pallas_call(
        kernel,
        out_shape=jax.ShapeDtypeStruct((QUARTER, D), bf16),
        in_specs=[hbm] * 7,
        out_specs=vmem,
        scratch_shapes=[
            raw,
            raw,
            raw,
            V((HEADS, TOK), f32),
            V((HEADS, DH), f32),
            V((1, D), f32),
            V((QUARTER, D), bf16),
            V((HEADS, TOK, 2 * DH), bf16),
            V((HEADS, DH, 4 * DH), bf16),
            V((HEADS, DH, 2 * DH), bf16),
            V((HEADS, DH, TOK), bf16),
            state,
            state,
            state,
            V((HEADS, 8, TOK), f32),
            V((HEADS, 8, TOK), f32),
            V((HEADS, DH, DH), f32),
            V((QUARTER, D), f32),
            raw,
            V((Y, HEADS, QUARTER, DH), bf16),
            *comm(80, V((COL, 16, DH), f32), V((COL, 8, DH), f32)),
            *comm(128, col, col),
            pltpu.SemaphoreType.DMA((4, 7)),
            pltpu.SemaphoreType.DMA((4, 7)),
            pltpu.SemaphoreType.DMA((4, 7)),
            pltpu.SemaphoreType.DMA((4, 7)),
            pltpu.SemaphoreType.DMA((HEADS, Y - 1)),
            pltpu.SemaphoreType.DMA((HEADS, Y - 1)),
            pltpu.SemaphoreType.DMA((28,)),
        ],
        compiler_params=pltpu.CompilerParams(
            collective_id=0, has_side_effects=True, vmem_limit_bytes=56 << 20
        ),
    )(queries, key_rows, values, write_gate.T, ridge_diag, norm_gain.reshape(1, D), gate_logits)


def solution(mesh):
    return jax.shard_map(
        shards,
        mesh=mesh,
        in_specs=(
            P("seq", "head"),
            P("seq", "head"),
            P("seq", "head"),
            P("seq", "head"),
            P("head", None),
            P(),
            P(("seq", "head"), None),
        ),
        out_specs=P(("seq", "head"), None),
        check_vma=False,
    )
```

```python
import functools

import jax
import jax.numpy as jnp
from jax import lax
from jax.experimental import pallas as pl
from jax.experimental.pallas import tpu as pltpu
from jax.sharding import PartitionSpec as P

MESH = pl.DeviceIdType.MESH
f32, bf16 = jnp.float32, jnp.bfloat16
ITERS = 8
HEADS = 8
DH = 128
TOK = 256
ROW = 8
COL = 8
Y = 4
QUARTER = TOK // Y
D = Y * HEADS * DH
EPS = 1e-6
FIRST, LAST = (0, 1), (2, 3, 6, 7, 4, 5)
FINISH = ((2, 3), (6, 7), (4, 5))


def dot(a, b):
    return jnp.dot(a, b, preferred_element_type=f32)


def sums(x):
    return jnp.sum(x, axis=0, keepdims=True)


def split(x):
    hi = x.astype(bf16)
    return hi, (x - hi.astype(f32)).astype(bf16)


def stack(x):
    return jnp.concatenate(split(x), axis=0)


def iota(shape, axis):
    return lax.broadcasted_iota(jnp.int32, shape, axis)


def causal(scores, tri):
    top = jnp.concatenate([jnp.where(tri, scores[0:128, 0:128], 0.0), scores[0:128, 128:256]], axis=1)
    bottom = jnp.concatenate(
        [jnp.zeros((128, 128), f32), jnp.where(tri, scores[128:256, 128:256], 0.0)], axis=1
    )
    return jnp.concatenate([top, bottom], axis=0)


def diag_rows(d):
    hi = d.astype(bf16).astype(f32)
    row = iota((16, 128), 0)
    return jnp.where(row == 0, hi, jnp.where(row == 1, d - hi, 0.0)).astype(bf16)


def diag_of(rows):
    return rows[0:1] + rows[1:2]


def flip(a, s):
    for bit in (1, 2, 4):
        if s & bit:
            a = a + bit - 2 * bit * ((a // bit) % 2)
    return a


def pack(state):
    row, lane = iota((64, 128), 0), iota((64, 128), 1)
    low = pltpu.roll(state[64:128], 64, 1)
    return jnp.where(lane > row, state[0:64], jnp.where(lane < row, low, 0.0))


def unpack(half):
    row, lane = iota((64, 128), 0), iota((64, 128), 1)
    low = pltpu.roll(jnp.where(lane < row, half, 0.0), 64, 1)
    upper = jnp.concatenate([jnp.where(lane > row, half, 0.0), low], axis=0)
    return upper + upper.T


def kernel(
    q, k, v, wgt, ridge, gain, gate, out,
    kbuf, qbuf, vbuf, wbuf, rbuf, nbuf, gbuf,
    keys2, mix, gg, vct, r, p, x, rr, cvs, dgb, sg, mesa, full,
    snd_k, row_k, e_k, cs_k, cr_k, zs_k, zr_k, s4_k, all_k,
    snd_v, row_v, e_v, cs_v, cr_v, zs_v, zr_v, s4_v, all_v,
    rs_s, rs_r, cs_s, cs_r, os_s, os_r, loc,
):
    seq, y = lax.axis_index("seq"), lax.axis_index("head")
    z, me = seq // ROW, seq % ROW
    heads = [flip(me, s) for s in range(HEADS)]

    barrier = pltpu.get_barrier_semaphore()
    for i in range(1, ROW):
        pl.semaphore_signal(barrier, inc=1, device_id=(z * ROW + heads[i], y), device_id_type=MESH)
    for i in range(1, COL):
        pl.semaphore_signal(barrier, inc=1, device_id=(flip(z, i) * ROW + me, y), device_id_type=MESH)
    for i in range(1, Y):
        pl.semaphore_signal(barrier, inc=1, device_id=(seq, flip(y, i)), device_id_type=MESH)

    def columns(ref, s):
        return ref.at[:, pl.ds(pl.multiple_of(heads[s] * DH, DH), DH)]

    local = {}

    def fetch(name, src, dst):
        local[name] = pltpu.make_async_copy(src, dst, loc.at[len(local)])
        local[name].start()

    fetch("w", wgt, wbuf)
    for s in ORDER:
        fetch(("k", s), columns(k, s), kbuf.at[s])
    started = []

    def start(src, dst, ssem, rsem, device):
        copy = pltpu.make_async_remote_copy(
            src_ref=src, dst_ref=dst, send_sem=ssem, recv_sem=rsem, device_id=device, device_id_type=MESH
        )
        copy.start()
        started.append(copy)
        return copy

    def to_row(stage, s, src, dst):
        sems = rs_s.at[stage, s - 1], rs_r.at[stage, s - 1]
        return start(src.at[s], dst.at[s], *sems, (z * ROW + heads[s], y))

    def to_col(stage, src, dst):
        return [
            start(
                src.at[flip(z, i)],
                dst.at[z],
                cs_s.at[stage, i - 1],
                cs_r.at[stage, i - 1],
                (flip(z, i) * ROW + me, y),
            )
            for i in (4, 5, 3, 6, 2, 1, 7)
        ]

    eye = iota((128, 128), 0) == iota((128, 128), 1)
    tri = iota((128, 128), 0) <= iota((128, 128), 1)

    local["w"].wait()
    wait_k1 = []
    for batch in (ORDER[:3], ORDER[3:]):
        for s in batch:
            local["k", s].wait()
        keys_t = [kbuf[s].astype(f32).T for s in batch]
        invs = [lax.rsqrt(sums(k_t * k_t) + EPS) for k_t in keys_t]
        gates = [wbuf[pl.ds(heads[s], 1), :] * inv for s, inv in zip(batch, invs)]
        weighed = [(k_t * (cv * inv)).astype(bf16) for k_t, cv, inv in zip(keys_t, gates, invs)]
        states = [dot(kc_t, kbuf[s]) for s, kc_t in zip(batch, weighed)]
        for s, state in zip(batch, states):
            snd_k[s, 0:64] = pack(state).astype(bf16)
            snd_k[s, 64:80] = diag_rows(sums(jnp.where(eye, state, 0.0)))
        for s, cv, kc_t in zip(batch, gates, weighed):
            cvs[s] = jnp.broadcast_to(cv, (8, TOK))
            mix[s, :, 256:512] = kc_t
        if batch[0] == ORDER[0]:
            pl.semaphore_wait(barrier, ROW + COL + Y - 3)
        for s in batch:
            if s:
                wait_k1.append(to_row(0, s, snd_k, row_k))
        for s in batch:
            fetch(("v", s), columns(v, s), vbuf.at[s])
    row_k[0] = snd_k[0]
    for s in range(HEADS):
        fetch(("q", s), columns(q, s), qbuf.at[s])
    fetch("r", ridge, rbuf)
    fetch("n", gain, nbuf)
    fetch("g", gate, gbuf)
    wait_v1 = []
    for batch in (ORDER,):
        for s in batch:
            local["v", s].wait()
        weighed = [(vbuf[s].astype(f32).T * cvs[s, 0:1]).astype(bf16) for s in batch]
        states = [dot(vc_t, kbuf[s]) for s, vc_t in zip(batch, weighed)]
        for s, vc_t, state in zip(batch, weighed, states):
            vct[s] = vc_t
            snd_v[s] = state.astype(bf16)
        for s in batch:
            if s:
                wait_v1.append(to_row(1, s, snd_v, row_v))
    row_v[0] = snd_v[0]

    def row_sums(waits, rows, e, pieces, landed, stage, with_diag):
        for copy in waits:
            copy.wait_recv()
        total = rows[0].astype(f32)
        for b in range(1, ROW):
            total = total + rows[b].astype(f32)
        for j in range(COL):
            if with_diag:
                pieces[j, 0:8] = total[8 * j : 8 * j + 8]
                pieces[j, 8:16] = jnp.broadcast_to(diag_of(total[64:80]), (8, 128))
            else:
                pieces[j] = total[16 * j : 16 * j + 16].astype(bf16)
        landed[z] = pieces[z]
        copies = to_col(stage, pieces, landed)
        total = jnp.zeros(e.shape[1:], f32)
        for b in range(ROW):
            e[b] = total
            if b < ROW - 1:
                total = total + rows[flip(me, b)].astype(f32)
        return copies

    def col_sums(waits, landed, zs, zr, stage):
        for copy in waits:
            copy.wait_recv()
        rows = zs.shape[1]
        total = jnp.zeros((rows, 128), f32)
        for b in range(COL):
            zs[b] = total.astype(zs.dtype)
            total = total + landed[b, 0:rows].astype(f32)
        zr[z] = zs[z]
        return to_col(stage, zs, zr)

    def hand_out(waits, zr, e, s4, everything, stage, diag):
        for copy in waits:
            copy.wait_recv()
        before = jnp.concatenate([zr[j].astype(f32) for j in range(COL)], axis=0)
        copies = {}
        for batch in ((1, 4, 5, 2), (3, 6, 7, 0)):
            for s in batch:
                row = e[heads[s]]
                rows = before.shape[0]
                s4[s, 0:rows] = (before + row[0:rows]).astype(bf16)
                if diag is not None:
                    s4[s, 64:80] = diag_rows(diag + diag_of(row[64:80]))
            for s in batch:
                if s:
                    copies[s] = to_row(stage, s, s4, everything)
        everything[0] = s4[0]
        return copies

    wait_k2 = row_sums(wait_k1, row_k, e_k, cs_k, cr_k, 0, True)
    wait_v2 = row_sums(wait_v1, row_v, e_v, cs_v, cr_v, 1, False)

    for s in range(HEADS):
        local["q", s].wait()
        q_t = qbuf[s].astype(f32).T
        q_t = q_t * lax.rsqrt(sums(q_t * q_t) + EPS)
        r[s] = q_t
        p[s] = q_t
        x[s] = jnp.zeros((DH, TOK), f32)
        rr[s] = jnp.broadcast_to(sums(q_t * q_t), (8, TOK))
        keys2[s, :, 0:128] = kbuf[s]
        keys2[s, :, 128:256] = kbuf[s]
    wait_k3 = col_sums(wait_k2, cr_k, zs_k, zr_k, 2)
    wait_v3 = col_sums(wait_v2, cr_v, zs_v, zr_v, 3)
    diag = jnp.zeros((1, 128), f32)
    for b in range(COL):
        diag = diag + jnp.where(b < z, cr_k[b, 8:9], 0.0)
    for name in ("r", "n", "g"):
        local[name].wait()
    for j in range(Y):
        part = slice(1024 * j, 1024 * j + 1024)
        sg[:, part] = nbuf[:, part] * jax.nn.sigmoid(gbuf[:, part].astype(f32))
    wait_k4 = hand_out(wait_k3, zr_k, e_k, s4_k, all_k, 2, diag)

    def apply(s, direction):
        pp = stack(direction)
        inner = causal(dot(keys2[s], pp), tri).astype(bf16)
        d = dgb[s]
        return dot(mix[s], jnp.concatenate([pp, inner], axis=0)) + jnp.concatenate([d, d], axis=1) * direction

    def place_states(slots):
        for s in slots:
            if s:
                wait_k4[s].wait_recv()
        for s in slots:
            before = unpack(all_k[s, 0:64].astype(f32)).astype(bf16)
            mix[s, :, 0:128] = before
            mix[s, :, 128:256] = before
            d = diag_of(all_k[s, 64:80].astype(f32)) + rbuf[pl.ds(heads[s], 1), :]
            dgb[s] = jnp.broadcast_to(jnp.sum(jnp.where(eye, d, 0.0), axis=1, keepdims=True), (128, 128))

    def sweep(slots):
        images = [apply(s, p[s]) for s in slots]
        for s, image in zip(slots, images):
            direction, norm_now = p[s], rr[s][0:1]
            alpha = norm_now / sums(direction * image)
            x[s] = x[s] + alpha * direction
            residual = r[s] - alpha * image
            r[s] = residual
            norm_next = sums(residual * residual)
            p[s] = residual + (norm_next / norm_now) * direction
            rr[s] = jnp.broadcast_to(norm_next, (8, TOK))

    def sweeps(slots, count):
        def step(n, carry):
            sweep(slots)
            return carry

        lax.fori_loop(0, count, step, 0, unroll=True)

    wait_out = []

    def solution_of(slots):
        images = [apply(s, p[s]) for s in slots]
        return [stack(x[s] + (rr[s][0:1] / sums(p[s] * image)) * p[s]) for s, image in zip(slots, images)]

    def attention(slots, found):
        return [causal(dot(keys2[s], xx), tri).astype(bf16) for s, xx in zip(slots, found)]

    def place_values(slots):
        for s in slots:
            if s:
                wait_v4[s].wait_recv()
            gg[s, :, 0:128] = all_v[s]
            gg[s, :, 128:256] = all_v[s]

    def results(slots, found, inner):
        outs = [
            dot(jnp.concatenate([gg[s], vct[s]], axis=1), jnp.concatenate([xx, scores], axis=0))
            for s, xx, scores in zip(slots, found, inner)
        ]
        for s, result in zip(slots, outs):
            mesa[s] = result.T.astype(bf16)

    def send_out(slots):
        for s in slots:
            for i in (2, 1, 3):
                to = flip(y, i)
                wait_out.append(
                    start(
                        mesa.at[s, pl.ds(pl.multiple_of(to * QUARTER, QUARTER), QUARTER), :],
                        full.at[y, heads[s]],
                        os_s.at[s, i - 1],
                        os_r.at[s, i - 1],
                        (seq, to),
                    )
                )
            full[y, heads[s]] = mesa[s, pl.ds(pl.multiple_of(y * QUARTER, QUARTER), QUARTER), :]

    wait_v4 = hand_out(wait_v3, zr_v, e_v, s4_v, all_v, 3, None)
    place_states(FIRST)
    sweeps(FIRST, ITERS - 3)
    place_states(LAST)
    sweep(FIRST + LAST)
    sweep(FIRST + LAST)
    found = solution_of(FIRST)
    sweep(LAST)
    inner = attention(FIRST, found)
    sweep(LAST)
    place_values(FIRST)
    results(FIRST, found, inner)
    sweep(LAST)
    send_out(FIRST)
    sweeps(LAST, ITERS - 6)
    place_values(LAST)
    for slots in FINISH:
        found = solution_of(slots)
        results(slots, found, attention(slots, found))
        send_out(slots)

    square = jnp.zeros((QUARTER, DH), f32)
    for slots in (FIRST, *FINISH):
        for copy in wait_out[: 3 * len(slots)]:
            copy.wait_recv()
        del wait_out[: 3 * len(slots)]
        for s in slots:
            for i in range(Y):
                part = full[flip(y, i), heads[s]].astype(f32)
                square = square + part * part
    factor = lax.rsqrt(jnp.sum(square, axis=1, keepdims=True) * (1.0 / D) + EPS)
    for j in range(Y):
        for h in range(HEADS):
            cols = slice((j * HEADS + h) * DH, (j * HEADS + h + 1) * DH)
            out[:, cols] = (full[j, h].astype(f32) * factor * sg[:, cols]).astype(bf16)
    for copy in started:
        copy.wait_send()


ORDER = (4, 5, 2, 3, 6, 7, 1, 0)


def shards(queries, key_rows, values, write_gate, ridge_diag, norm_gain, gate_logits):
    V = pltpu.VMEM
    raw = V((HEADS, TOK, DH), bf16)
    state = V((HEADS, DH, TOK), f32)
    col = V((COL, 16, DH), bf16)

    def comm(rows, piece, back):
        sent = V((ROW, rows, DH), bf16)
        return sent, sent, V((ROW, rows, DH), f32), piece, piece, back, back, sent, sent

    hbm, vmem = pl.BlockSpec(memory_space=pltpu.HBM), pl.BlockSpec(memory_space=pltpu.VMEM)
    return pl.pallas_call(
        kernel,
        out_shape=jax.ShapeDtypeStruct((QUARTER, D), bf16),
        in_specs=[hbm] * 7,
        out_specs=vmem,
        scratch_shapes=[
            raw,
            raw,
            raw,
            V((HEADS, TOK), f32),
            V((HEADS, DH), f32),
            V((1, D), f32),
            V((QUARTER, D), bf16),
            V((HEADS, TOK, 2 * DH), bf16),
            V((HEADS, DH, 4 * DH), bf16),
            V((HEADS, DH, 2 * DH), bf16),
            V((HEADS, DH, TOK), bf16),
            state,
            state,
            state,
            V((HEADS, 8, TOK), f32),
            V((HEADS, 8, TOK), f32),
            V((HEADS, DH, DH), f32),
            V((QUARTER, D), f32),
            raw,
            V((Y, HEADS, QUARTER, DH), bf16),
            *comm(80, V((COL, 16, DH), f32), V((COL, 8, DH), f32)),
            *comm(128, col, col),
            pltpu.SemaphoreType.DMA((4, 7)),
            pltpu.SemaphoreType.DMA((4, 7)),
            pltpu.SemaphoreType.DMA((4, 7)),
            pltpu.SemaphoreType.DMA((4, 7)),
            pltpu.SemaphoreType.DMA((HEADS, Y - 1)),
            pltpu.SemaphoreType.DMA((HEADS, Y - 1)),
            pltpu.SemaphoreType.DMA((28,)),
        ],
        compiler_params=pltpu.CompilerParams(
            collective_id=0, has_side_effects=True, vmem_limit_bytes=56 << 20
        ),
    )(queries, key_rows, values, write_gate.T, ridge_diag, norm_gain.reshape(1, D), gate_logits)


def solution(mesh):
    return jax.shard_map(
        shards,
        mesh=mesh,
        in_specs=(
            P("seq", "head"),
            P("seq", "head"),
            P("seq", "head"),
            P("seq", "head"),
            P("head", None),
            P(),
            P(("seq", "head"), None),
        ),
        out_specs=P(("seq", "head"), None),
        check_vma=False,
    )
```

```python
import functools

import jax
import jax.numpy as jnp
from jax import lax
from jax.experimental import pallas as pl
from jax.experimental.pallas import tpu as pltpu
from jax.sharding import PartitionSpec as P

MESH = pl.DeviceIdType.MESH
f32, bf16 = jnp.float32, jnp.bfloat16
ITERS = 8
HEADS = 8
DH = 128
TOK = 256
ROW = 8
COL = 8
Y = 4
QUARTER = TOK // Y
D = Y * HEADS * DH
EPS = 1e-6
FIRST, LAST = (0, 1), (2, 3, 6, 7, 4, 5)
FINISH = ((2, 3), (6, 7), (4, 5))


def dot(a, b):
    return jnp.dot(a, b, preferred_element_type=f32)


def sums(x):
    return jnp.sum(x, axis=0, keepdims=True)


def split(x):
    hi = x.astype(bf16)
    return hi, (x - hi.astype(f32)).astype(bf16)


def stack(x):
    return jnp.concatenate(split(x), axis=0)


def iota(shape, axis):
    return lax.broadcasted_iota(jnp.int32, shape, axis)


def causal(scores, tri):
    top = jnp.concatenate([jnp.where(tri, scores[0:128, 0:128], 0.0), scores[0:128, 128:256]], axis=1)
    bottom = jnp.concatenate(
        [jnp.zeros((128, 128), f32), jnp.where(tri, scores[128:256, 128:256], 0.0)], axis=1
    )
    return jnp.concatenate([top, bottom], axis=0)


def diag_rows(d):
    hi = d.astype(bf16).astype(f32)
    row = iota((16, 128), 0)
    return jnp.where(row == 0, hi, jnp.where(row == 1, d - hi, 0.0)).astype(bf16)


def diag_of(rows):
    return rows[0:1] + rows[1:2]


def flip(a, s):
    for bit in (1, 2, 4):
        if s & bit:
            a = a + bit - 2 * bit * ((a // bit) % 2)
    return a


def pack(state):
    row, lane = iota((64, 128), 0), iota((64, 128), 1)
    low = pltpu.roll(state[64:128], 64, 1)
    return jnp.where(lane > row, state[0:64], jnp.where(lane < row, low, 0.0))


def unpack(half):
    row, lane = iota((64, 128), 0), iota((64, 128), 1)
    low = pltpu.roll(jnp.where(lane < row, half, 0.0), 64, 1)
    upper = jnp.concatenate([jnp.where(lane > row, half, 0.0), low], axis=0)
    return upper + upper.T


def kernel(
    q, k, v, wgt, ridge, gain, gate, out,
    kbuf, qbuf, vbuf, wbuf, rbuf, nbuf, gbuf,
    keys2, mix, gg, vct, r, p, x, rr, cvs, dgb, sg, mesa, full,
    snd_k, row_k, e_k, cs_k, cr_k, zs_k, zr_k, s4_k, all_k,
    snd_v, row_v, e_v, cs_v, cr_v, zs_v, zr_v, s4_v, all_v,
    rs_s, rs_r, cs_s, cs_r, os_s, os_r, loc,
):
    seq, y = lax.axis_index("seq"), lax.axis_index("head")
    z, me = seq // ROW, seq % ROW
    heads = [flip(me, s) for s in range(HEADS)]

    barrier = pltpu.get_barrier_semaphore()
    for i in range(1, ROW):
        pl.semaphore_signal(barrier, inc=1, device_id=(z * ROW + heads[i], y), device_id_type=MESH)
    for i in range(1, COL):
        pl.semaphore_signal(barrier, inc=1, device_id=(flip(z, i) * ROW + me, y), device_id_type=MESH)
    for i in range(1, Y):
        pl.semaphore_signal(barrier, inc=1, device_id=(seq, flip(y, i)), device_id_type=MESH)

    def columns(ref, s):
        return ref.at[:, pl.ds(pl.multiple_of(heads[s] * DH, DH), DH)]

    local = {}

    def fetch(name, src, dst):
        local[name] = pltpu.make_async_copy(src, dst, loc.at[len(local)])
        local[name].start()

    fetch("w", wgt, wbuf)
    for s in ORDER:
        fetch(("k", s), columns(k, s), kbuf.at[s])
    started = []

    def start(src, dst, ssem, rsem, device):
        copy = pltpu.make_async_remote_copy(
            src_ref=src, dst_ref=dst, send_sem=ssem, recv_sem=rsem, device_id=device, device_id_type=MESH
        )
        copy.start()
        started.append(copy)
        return copy

    def to_row(stage, s, src, dst):
        sems = rs_s.at[stage, s - 1], rs_r.at[stage, s - 1]
        return start(src.at[s], dst.at[s], *sems, (z * ROW + heads[s], y))

    def to_col(stage, src, dst):
        return [
            start(
                src.at[flip(z, i)],
                dst.at[z],
                cs_s.at[stage, i - 1],
                cs_r.at[stage, i - 1],
                (flip(z, i) * ROW + me, y),
            )
            for i in (4, 5, 3, 6, 2, 1, 7)
        ]

    eye = iota((128, 128), 0) == iota((128, 128), 1)
    tri = iota((128, 128), 0) <= iota((128, 128), 1)

    local["w"].wait()
    wait_k1 = []
    for batch in (ORDER[:3], ORDER[3:]):
        for s in batch:
            local["k", s].wait()
        keys_t = [kbuf[s].astype(f32).T for s in batch]
        invs = [lax.rsqrt(sums(k_t * k_t) + EPS) for k_t in keys_t]
        gates = [wbuf[pl.ds(heads[s], 1), :] * inv for s, inv in zip(batch, invs)]
        weighed = [(k_t * (cv * inv)).astype(bf16) for k_t, cv, inv in zip(keys_t, gates, invs)]
        states = [dot(kc_t, kbuf[s]) for s, kc_t in zip(batch, weighed)]
        for s, state in zip(batch, states):
            snd_k[s, 0:64] = pack(state).astype(bf16)
            snd_k[s, 64:80] = diag_rows(sums(jnp.where(eye, state, 0.0)))
        for s, cv, kc_t in zip(batch, gates, weighed):
            cvs[s] = jnp.broadcast_to(cv, (8, TOK))
            mix[s, :, 256:512] = kc_t
        if batch[0] == ORDER[0]:
            pl.semaphore_wait(barrier, ROW + COL + Y - 3)
        for s in batch:
            if s:
                wait_k1.append(to_row(0, s, snd_k, row_k))
        for s in batch:
            fetch(("v", s), columns(v, s), vbuf.at[s])
    row_k[0] = snd_k[0]
    for s in range(HEADS):
        fetch(("q", s), columns(q, s), qbuf.at[s])
    fetch("r", ridge, rbuf)
    fetch("n", gain, nbuf)
    fetch("g", gate, gbuf)
    wait_v1 = []
    for batch in (ORDER,):
        for s in batch:
            local["v", s].wait()
        weighed = [(vbuf[s].astype(f32).T * cvs[s, 0:1]).astype(bf16) for s in batch]
        states = [dot(vc_t, kbuf[s]) for s, vc_t in zip(batch, weighed)]
        for s, vc_t, state in zip(batch, weighed, states):
            vct[s] = vc_t
            snd_v[s] = state.astype(bf16)
        for s in batch:
            if s:
                wait_v1.append(to_row(1, s, snd_v, row_v))
    row_v[0] = snd_v[0]

    def row_sums(waits, rows, e, pieces, landed, stage, with_diag):
        for copy in waits:
            copy.wait_recv()
        total = rows[0].astype(f32)
        for b in range(1, ROW):
            total = total + rows[b].astype(f32)
        for j in range(COL):
            if with_diag:
                pieces[j, 0:8] = total[8 * j : 8 * j + 8]
                pieces[j, 8:16] = jnp.broadcast_to(diag_of(total[64:80]), (8, 128))
            else:
                pieces[j] = total[16 * j : 16 * j + 16].astype(bf16)
        landed[z] = pieces[z]
        copies = to_col(stage, pieces, landed)
        total = jnp.zeros(e.shape[1:], f32)
        for b in range(ROW):
            e[b] = total
            if b < ROW - 1:
                total = total + rows[flip(me, b)].astype(f32)
        return copies

    def col_sums(waits, landed, zs, zr, stage):
        for copy in waits:
            copy.wait_recv()
        rows = zs.shape[1]
        total = jnp.zeros((rows, 128), f32)
        for b in range(COL):
            zs[b] = total.astype(zs.dtype)
            total = total + landed[b, 0:rows].astype(f32)
        zr[z] = zs[z]
        return to_col(stage, zs, zr)

    def hand_out(waits, zr, e, s4, everything, stage, diag):
        for copy in waits:
            copy.wait_recv()
        before = jnp.concatenate([zr[j].astype(f32) for j in range(COL)], axis=0)
        copies = {}
        for batch in ((1, 4, 5, 2, 3, 6, 7, 0),):
            for s in batch:
                row = e[heads[s]]
                rows = before.shape[0]
                s4[s, 0:rows] = (before + row[0:rows]).astype(bf16)
                if diag is not None:
                    s4[s, 64:80] = diag_rows(diag + diag_of(row[64:80]))
            for s in batch:
                if s:
                    copies[s] = to_row(stage, s, s4, everything)
        everything[0] = s4[0]
        return copies

    wait_k2 = row_sums(wait_k1, row_k, e_k, cs_k, cr_k, 0, True)
    wait_v2 = row_sums(wait_v1, row_v, e_v, cs_v, cr_v, 1, False)

    for s in range(HEADS):
        local["q", s].wait()
    for s in range(HEADS):
        q_t = qbuf[s].astype(f32).T
        q_t = q_t * lax.rsqrt(sums(q_t * q_t) + EPS)
        r[s] = q_t
        p[s] = q_t
        x[s] = jnp.zeros((DH, TOK), f32)
        rr[s] = jnp.broadcast_to(sums(q_t * q_t), (8, TOK))
        keys2[s, :, 0:128] = kbuf[s]
        keys2[s, :, 128:256] = kbuf[s]
    wait_k3 = col_sums(wait_k2, cr_k, zs_k, zr_k, 2)
    wait_v3 = col_sums(wait_v2, cr_v, zs_v, zr_v, 3)
    diag = jnp.zeros((1, 128), f32)
    for b in range(COL):
        diag = diag + jnp.where(b < z, cr_k[b, 8:9], 0.0)
    for name in ("r", "n", "g"):
        local[name].wait()
    for j in range(Y):
        part = slice(1024 * j, 1024 * j + 1024)
        sg[:, part] = nbuf[:, part] * jax.nn.sigmoid(gbuf[:, part].astype(f32))
    wait_k4 = hand_out(wait_k3, zr_k, e_k, s4_k, all_k, 2, diag)

    def apply(s, direction):
        pp = stack(direction)
        inner = causal(dot(keys2[s], pp), tri).astype(bf16)
        d = dgb[s]
        return dot(mix[s], jnp.concatenate([pp, inner], axis=0)) + jnp.concatenate([d, d], axis=1) * direction

    def place_states(slots):
        for s in slots:
            if s:
                wait_k4[s].wait_recv()
        for s in slots:
            before = unpack(all_k[s, 0:64].astype(f32)).astype(bf16)
            mix[s, :, 0:128] = before
            mix[s, :, 128:256] = before
            d = diag_of(all_k[s, 64:80].astype(f32)) + rbuf[pl.ds(heads[s], 1), :]
            dgb[s] = jnp.broadcast_to(jnp.sum(jnp.where(eye, d, 0.0), axis=1, keepdims=True), (128, 128))

    def sweep(slots):
        images = [apply(s, p[s]) for s in slots]
        for s, image in zip(slots, images):
            direction, norm_now = p[s], rr[s][0:1]
            alpha = norm_now / sums(direction * image)
            x[s] = x[s] + alpha * direction
            residual = r[s] - alpha * image
            r[s] = residual
            norm_next = sums(residual * residual)
            p[s] = residual + (norm_next / norm_now) * direction
            rr[s] = jnp.broadcast_to(norm_next, (8, TOK))

    def sweeps(slots, count):
        def step(n, carry):
            sweep(slots)
            return carry

        lax.fori_loop(0, count, step, 0, unroll=True)

    wait_out = []

    def solution_of(slots):
        images = [apply(s, p[s]) for s in slots]
        return [stack(x[s] + (rr[s][0:1] / sums(p[s] * image)) * p[s]) for s, image in zip(slots, images)]

    def attention(slots, found):
        return [causal(dot(keys2[s], xx), tri).astype(bf16) for s, xx in zip(slots, found)]

    def place_values(slots):
        for s in slots:
            if s:
                wait_v4[s].wait_recv()
            gg[s, :, 0:128] = all_v[s]
            gg[s, :, 128:256] = all_v[s]

    def results(slots, found, inner):
        outs = [
            dot(jnp.concatenate([gg[s], vct[s]], axis=1), jnp.concatenate([xx, scores], axis=0))
            for s, xx, scores in zip(slots, found, inner)
        ]
        for s, result in zip(slots, outs):
            mesa[s] = result.T.astype(bf16)

    def send_out(slots):
        for s in slots:
            for i in (2, 1, 3):
                to = flip(y, i)
                wait_out.append(
                    start(
                        mesa.at[s, pl.ds(pl.multiple_of(to * QUARTER, QUARTER), QUARTER), :],
                        full.at[y, heads[s]],
                        os_s.at[s, i - 1],
                        os_r.at[s, i - 1],
                        (seq, to),
                    )
                )
            full[y, heads[s]] = mesa[s, pl.ds(pl.multiple_of(y * QUARTER, QUARTER), QUARTER), :]

    wait_v4 = hand_out(wait_v3, zr_v, e_v, s4_v, all_v, 3, None)
    place_states(FIRST)
    sweeps(FIRST, ITERS - 3)
    place_states(LAST)
    sweep(FIRST + LAST)
    sweep(FIRST + LAST)
    found = solution_of(FIRST)
    sweep(LAST)
    inner = attention(FIRST, found)
    sweep(LAST)
    place_values(FIRST)
    results(FIRST, found, inner)
    sweep(LAST)
    send_out(FIRST)
    sweeps(LAST, ITERS - 6)
    place_values(LAST)
    for slots in FINISH:
        found = solution_of(slots)
        results(slots, found, attention(slots, found))
        send_out(slots)

    square = jnp.zeros((QUARTER, DH), f32)
    for slots in (FIRST, *FINISH):
        for copy in wait_out[: 3 * len(slots)]:
            copy.wait_recv()
        del wait_out[: 3 * len(slots)]
        for s in slots:
            for i in range(Y):
                part = full[flip(y, i), heads[s]].astype(f32)
                square = square + part * part
    factor = lax.rsqrt(jnp.sum(square, axis=1, keepdims=True) * (1.0 / D) + EPS)
    for j in range(Y):
        for h in range(HEADS):
            cols = slice((j * HEADS + h) * DH, (j * HEADS + h + 1) * DH)
            out[:, cols] = (full[j, h].astype(f32) * factor * sg[:, cols]).astype(bf16)
    for copy in started:
        copy.wait_send()


ORDER = (4, 5, 2, 3, 6, 7, 1, 0)


def shards(queries, key_rows, values, write_gate, ridge_diag, norm_gain, gate_logits):
    V = pltpu.VMEM
    raw = V((HEADS, TOK, DH), bf16)
    state = V((HEADS, DH, TOK), f32)
    col = V((COL, 16, DH), bf16)

    def comm(rows, piece, back):
        sent = V((ROW, rows, DH), bf16)
        return sent, sent, V((ROW, rows, DH), f32), piece, piece, back, back, sent, sent

    hbm, vmem = pl.BlockSpec(memory_space=pltpu.HBM), pl.BlockSpec(memory_space=pltpu.VMEM)
    return pl.pallas_call(
        kernel,
        out_shape=jax.ShapeDtypeStruct((QUARTER, D), bf16),
        in_specs=[hbm] * 7,
        out_specs=vmem,
        scratch_shapes=[
            raw,
            raw,
            raw,
            V((HEADS, TOK), f32),
            V((HEADS, DH), f32),
            V((1, D), f32),
            V((QUARTER, D), bf16),
            V((HEADS, TOK, 2 * DH), bf16),
            V((HEADS, DH, 4 * DH), bf16),
            V((HEADS, DH, 2 * DH), bf16),
            V((HEADS, DH, TOK), bf16),
            state,
            state,
            state,
            V((HEADS, 8, TOK), f32),
            V((HEADS, 8, TOK), f32),
            V((HEADS, DH, DH), f32),
            V((QUARTER, D), f32),
            raw,
            V((Y, HEADS, QUARTER, DH), bf16),
            *comm(80, V((COL, 16, DH), f32), V((COL, 8, DH), f32)),
            *comm(128, col, col),
            pltpu.SemaphoreType.DMA((4, 7)),
            pltpu.SemaphoreType.DMA((4, 7)),
            pltpu.SemaphoreType.DMA((4, 7)),
            pltpu.SemaphoreType.DMA((4, 7)),
            pltpu.SemaphoreType.DMA((HEADS, Y - 1)),
            pltpu.SemaphoreType.DMA((HEADS, Y - 1)),
            pltpu.SemaphoreType.DMA((28,)),
        ],
        compiler_params=pltpu.CompilerParams(
            collective_id=0, has_side_effects=True, vmem_limit_bytes=56 << 20
        ),
    )(queries, key_rows, values, write_gate.T, ridge_diag, norm_gain.reshape(1, D), gate_logits)


def solution(mesh):
    return jax.shard_map(
        shards,
        mesh=mesh,
        in_specs=(
            P("seq", "head"),
            P("seq", "head"),
            P("seq", "head"),
            P("seq", "head"),
            P("head", None),
            P(),
            P(("seq", "head"), None),
        ),
        out_specs=P(("seq", "head"), None),
        check_vma=False,
    )
```
